32 devices in a mesh: seq: 8 (over z, x), tp: 4 (over y, core).
Axes of the slice: x: 2, y: 2, z: 4, core: 2. Of those that a mesh axis runs over, the one named last changes fastest.
Arguments:
- draft_q: bfloat16 [256, 4096], P('seq', 'tp'), may hold values from -16 to 16
- draft_kv: bfloat16 [2, 256, 4096], P(None, 'seq', 'tp'), may hold values from -6 to 6
- kv_pool: bfloat16 [2, 128, 128, 4096], P(None, 'seq', None, 'tp'), may hold values from -8 to 8
- page_table: int32 [4, 32], replicated, may hold values from -1 to 127, as said below
- cache_len: int32 [4], replicated, may hold values from 2048 to 4096, as said below
- tree_mask: int32 [4, 64, 64], replicated, may hold values from 0 to 1, as said below
- accepted_rows: int32 [4, 64], replicated, may hold values from -1 to 63, as said below
- out_weight: bfloat16 [4096, 4096], P('tp'), may hold values from -0.125 to 0.125
Outputs:
- layer_out: bfloat16 [256, 4096], P('seq', 'tp')
- accepted_kv: bfloat16 [2, 4, 128, 4096], P(None, None, None, 'tp')
The draws below stay inside these ranges and needn't reach their ends.
Inputs may be any that keep to these rules, and one draw needn't show every extreme that they name: `page_table`: entries past a request's cached pages are -1; the slots in use are distinct over all requests. `cache_len`: some request holds exactly 4096 cached tokens. `tree_mask`: entry (r, i, k) is 1 where draft row k is row i itself or one of its ancestors in request r's token tree; a parent precedes its children, row 0 is the root. `accepted_rows`: each row lists in ascending order the draft rows of one root-to-node path of the tree, then -1.
All inputs are finite; a program needn't handle non-finite values.
Results may differ from the reference program's by a relative error of at most 0.0051.
Values may be sent and summed in bfloat16 or wider, within the bound.
A program may use at most 128 MiB of HBM per device.

```python
import math
import jax
import jax.numpy as jnp
from jax import lax

D = 4096
HEADS = 32
HD = 128
PAGE = 128
CACHE_MAX = 4096
DRAFT = 64
REQ = 4
WIDTH = 4096
MAXP = 32
ROWS = 256
POOL = 128


def draw_layout(key):
    base_key = jax.random.fold_in(key, 11)
    key_len, key_long, key_perm = jax.random.split(base_key, 3)
    lengths = jax.random.randint(key_len, (REQ,), CACHE_MAX // 2, CACHE_MAX + 1)
    longest = jax.random.randint(key_long, (), 0, REQ)
    lengths = jnp.where(jnp.arange(REQ) == longest, CACHE_MAX, lengths).astype(jnp.int32)
    layout = jax.random.permutation(key_perm, POOL)[:REQ * MAXP].reshape(REQ, MAXP).astype(jnp.int32)
    first_slot = layout[longest, 0]
    top_slot = jnp.int32(POOL - 1)
    layout = jnp.where(layout == first_slot, top_slot, jnp.where(layout == top_slot, first_slot, layout))
    in_use = jnp.arange(MAXP)[None, :] * PAGE < lengths[:, None]
    layout = jnp.where(in_use, layout, -1).astype(jnp.int32)
    return (lengths, layout)


def draw_tree(key):
    base_key = jax.random.fold_in(key, 59)
    key_parent, key_node = jax.random.split(base_key)
    columns = jnp.arange(DRAFT)
    parent = jax.random.randint(key_parent, (REQ, DRAFT), 0, jnp.maximum(columns, 1)[None, :])
    identity = jnp.eye(DRAFT, dtype=jnp.int32)
    ancestry = jnp.broadcast_to(identity, (REQ, DRAFT, DRAFT))

    def grow(column, ancestry):
        above = ancestry[jnp.arange(REQ), parent[:, column]]
        fresh = jnp.maximum(above, identity[column][None, :])
        return ancestry.at[:, column].set(fresh)
    ancestry = lax.fori_loop(1, DRAFT, grow, ancestry)
    chosen = jax.random.randint(key_node, (REQ,), 0, DRAFT)
    chosen = jnp.where(jnp.arange(REQ) == 0, DRAFT - 1, chosen)
    on_chain = ancestry[jnp.arange(REQ), chosen]
    chain_rank = jnp.cumsum(on_chain, axis=1) - 1
    matches = (on_chain[:, None, :] == 1) & (chain_rank[:, None, :] == columns[None, :, None])
    chain_rows = jnp.sum(jnp.where(matches, columns[None, None, :], 0), axis=2)
    chain_count = jnp.sum(on_chain, axis=1)
    chain_rows = jnp.where(columns[None, :] < chain_count[:, None], chain_rows, -1)
    return (ancestry.astype(jnp.int32), chain_rows.astype(jnp.int32))


def draw_page_table(key, part):
    lengths, layout = draw_layout(key)
    return layout


def draw_cache_len(key, part):
    lengths, layout = draw_layout(key)
    return lengths


def draw_tree_mask(key, part):
    ancestry, chain_rows = draw_tree(key)
    return ancestry


def draw_accepted_rows(key, part):
    ancestry, chain_rows = draw_tree(key)
    return chain_rows


def draw_draft_q(key, part):
    key_main = jax.random.fold_in(jax.random.fold_in(key, 31), 0)
    queries = jax.random.normal(key_main, (ROWS, WIDTH))
    return jnp.clip(queries, -16.0, 16.0).astype(jnp.bfloat16)


def draw_kv_pool(key, part):
    key_main, key_scale = jax.random.split(jax.random.fold_in(key, 23))
    entries = jax.random.normal(key_main, (2, POOL, PAGE, WIDTH))
    key_scales = jnp.exp(jax.random.uniform(key_scale, (1, POOL, PAGE, 1), minval=math.log(0.3), maxval=math.log(3.0)))
    scales = jnp.concatenate([key_scales, jnp.ones_like(key_scales)], axis=0)
    entries = jnp.clip(entries * scales, -8.0, 8.0)
    return entries.astype(jnp.bfloat16)


def spiked(drawn, own_key, source, target, shards_of, factor):
    def block_of(dim):
        return (jnp.arange(drawn.shape[dim]) // (drawn.shape[dim] // shards_of)).reshape((-1,) + (1,) * (drawn.ndim - 1 - dim))

    near = jax.random.permutation(own_key, shards_of)[block_of(target)]
    other_side = (block_of(target) + shards_of // 2) % shards_of
    return jnp.where((block_of(source) == near) | (block_of(source) == other_side), factor * drawn, drawn)


def steps_of(own_key, dims, cuts, low, top_value):
    def one(dim, blocks):
        heights = jax.random.uniform(jax.random.fold_in(jax.random.fold_in(own_key, 6), dim), (blocks,), jnp.float32, low / len(cuts), top_value / len(cuts))
        return jnp.repeat(jnp.exp(heights), dims[dim] // blocks).reshape((-1,) + (1,) * (len(dims) - dim - 1))

    level = one(*cuts[0])
    for cut in cuts[1:]:
        level = level * one(*cut)
    return level


def bell_draw(stream_key, extent, width, limit, cuts=(), held_as=jnp.bfloat16):
    loudness = steps_of(stream_key, extent, cuts, -0.22, 0.18) if cuts else 1.0
    values = jax.random.normal(stream_key, extent, jnp.float32) * width * loudness
    return jnp.minimum(jnp.maximum(values, -limit), limit).astype(held_as)


def heavy_noise(stream_key, extent, scale, most, pieces, heavy, kind=jnp.bfloat16):
    drawn = scale * jax.random.normal(stream_key, extent, jnp.float32)
    if pieces:
        drawn = drawn * steps_of(stream_key, extent, pieces, -0.22, 0.18)
    return jnp.clip(spiked(drawn, jax.random.fold_in(stream_key, 3), *heavy), -most, most).astype(kind)


def setup_inputs(seed: int = 0) -> dict:
    key_of = jax.random.split(jax.random.key(seed), 9)
    return {
        "draft_q": draw_draft_q(jax.random.fold_in(key_of[8], 71), 0),
        "draft_kv": bell_draw(key_of[1], (2, ROWS, WIDTH), 1.0, 6.0, ((1, 8), (2, 4))),
        "kv_pool": draw_kv_pool(jax.random.fold_in(key_of[8], 71), 0),
        "page_table": draw_page_table(jax.random.fold_in(key_of[8], 71), 0),
        "cache_len": draw_cache_len(jax.random.fold_in(key_of[8], 71), 0),
        "tree_mask": draw_tree_mask(jax.random.fold_in(key_of[8], 71), 0),
        "accepted_rows": draw_accepted_rows(jax.random.fold_in(key_of[8], 71), 0),
        "out_weight": heavy_noise(key_of[7], (WIDTH, D), WIDTH ** -0.5, 0.125, ((0, 4),), (0, 1, 4, 2.0)),
    }


NEGATIVE = -1e+30

def block_stats(scores, allowed):
    masked = jnp.where(allowed, scores, NEGATIVE)
    block_max = lax.optimization_barrier(jnp.max(masked, axis=-1))
    weights = jnp.where(allowed, jnp.exp(masked - block_max[..., None]), 0.0)
    block_total = lax.optimization_barrier(jnp.sum(weights, axis=-1))
    rounded = lax.optimization_barrier(weights.astype(jnp.bfloat16)).astype(jnp.float32)
    return (block_max, block_total, rounded)

def reference(draft_q, draft_kv, kv_pool, page_table, cache_len, tree_mask, accepted_rows, out_weight):
    inv_root = 1.0 / math.sqrt(HD)
    highest = lax.Precision.HIGHEST

    def one_request(request):
        queries = lax.dynamic_slice_in_dim(draft_q, request * DRAFT, DRAFT, 0).astype(jnp.float32).reshape(DRAFT, HEADS, HD)
        slot_row = lax.dynamic_index_in_dim(page_table, request, 0, keepdims=False)
        safe_slots = jnp.maximum(slot_row, 0)
        page_keys = kv_pool[0][safe_slots].astype(jnp.float32).reshape(MAXP, PAGE, HEADS, HD)
        page_values = kv_pool[1][safe_slots].astype(jnp.float32).reshape(MAXP, PAGE, HEADS, HD)
        length = lax.dynamic_index_in_dim(cache_len, request, 0, keepdims=False)
        positions = jnp.arange(MAXP)[:, None] * PAGE + jnp.arange(PAGE)[None, :]
        is_live = (slot_row[:, None] >= 0) & (positions < length)
        scores = jnp.einsum('qhd,pthd->phqt', queries, page_keys, precision=highest) * inv_root
        page_max, page_total, page_weight = block_stats(scores, is_live[:, None, None, :])
        page_out = jnp.einsum('phqt,pthd->phqd', page_weight, page_values, precision=highest)
        draft_keys = lax.dynamic_slice_in_dim(draft_kv[0], request * DRAFT, DRAFT, 0).astype(jnp.float32).reshape(DRAFT, HEADS, HD)
        draft_values = lax.dynamic_slice_in_dim(draft_kv[1], request * DRAFT, DRAFT, 0).astype(jnp.float32).reshape(DRAFT, HEADS, HD)
        mask_rows = lax.dynamic_index_in_dim(tree_mask, request, 0, keepdims=False) == 1
        tree_scores = jnp.einsum('qhd,khd->hqk', queries, draft_keys, precision=highest) * inv_root
        tree_max, tree_total, tree_weight = block_stats(tree_scores, mask_rows[None, :, :])
        tree_out = jnp.einsum('hqk,khd->hqd', tree_weight, draft_values, precision=highest)
        row_top = jnp.maximum(lax.optimization_barrier(jnp.max(page_max, axis=0)), tree_max)
        page_factor = jnp.exp(page_max - row_top[None])
        tree_factor = jnp.exp(tree_max - row_top)
        numerator = lax.optimization_barrier(jnp.sum(page_factor[..., None] * page_out, axis=0)) + tree_factor[..., None] * tree_out
        denominator = lax.optimization_barrier(jnp.sum(page_factor * page_total, axis=0)) + tree_factor * tree_total
        attention = numerator / denominator[..., None]
        return jnp.transpose(attention, (1, 0, 2)).reshape(DRAFT, WIDTH).astype(jnp.bfloat16)
    attention_all = lax.map(one_request, jnp.arange(REQ)).reshape(ROWS, WIDTH)
    layer_out = jnp.dot(attention_all, out_weight, preferred_element_type=jnp.float32).astype(jnp.bfloat16)
    padded = jnp.concatenate([accepted_rows.astype(jnp.int32), jnp.full((REQ, PAGE - DRAFT), -1, jnp.int32)], axis=1)
    onehot = (padded[:, :, None] == jnp.arange(DRAFT).astype(jnp.int32)[None, None, :]).astype(jnp.float32)
    blocks = draft_kv.astype(jnp.float32).reshape(2, REQ, DRAFT, WIDTH)
    accepted_kv = jnp.einsum('rji,crid->crjd', onehot, blocks, precision=highest).astype(jnp.bfloat16)
    return (layer_out, accepted_kv)
```

```python
import functools
import math

import jax
import jax.numpy as jnp
from jax import lax
from jax.experimental import pallas as pl
from jax.experimental.pallas import tpu as pltpu
from jax.sharding import PartitionSpec as P

HD = 128
NEGATIVE = -1e30
MESH = pl.DeviceIdType.MESH
ANY = pl.BlockSpec(memory_space=pl.ANY)
VMEM = pl.BlockSpec(memory_space=pltpu.VMEM)
SMEM = pl.BlockSpec(memory_space=pltpu.SMEM)
NT = (((1,), (1,)), ((), ()))


def gather_kernel(n_req, group, q, kv, qa, kg, ssem, rsem, fsem, kssem, krsem, lsem):
    me = lax.axis_index("seq")
    grp = me // group
    inner = lax.rem(me, group)

    def across(d):
        return lax.rem(grp + d, n_req) * group + inner

    def mate(d):
        return lax.rem(inner + d, group)

    def other(d):
        return grp * group + mate(d)

    barrier = pltpu.get_barrier_semaphore()
    for d in range(1, n_req):
        pl.semaphore_signal(barrier, inc=1, device_id={"seq": across(d)}, device_id_type=MESH)
    for d in range(1, group):
        pl.semaphore_signal(barrier, inc=1, device_id={"seq": other(d)}, device_id_type=MESH)
    own_q = pltpu.make_async_copy(q, qa.at[me], lsem.at[0])
    own_kv = pltpu.make_async_copy(kv, kg.at[inner], lsem.at[1])
    own_q.start()
    own_kv.start()
    pl.semaphore_wait(barrier, n_req + group - 2)

    def send(src, dst, s, r, target):
        c = pltpu.make_async_remote_copy(
            src_ref=src, dst_ref=dst, send_sem=s, recv_sem=r,
            device_id={"seq": target}, device_id_type=MESH)
        c.start()
        return c

    sent = []
    for d in range(1, n_req):
        sent.append(send(q, qa.at[me], ssem.at[d - 1], rsem.at[me], across(d)))
    for d in range(1, group):
        sent.append(send(q, qa.at[me], ssem.at[n_req - 2 + d], rsem.at[me], other(d)))
    for d in range(1, group):
        sent.append(send(kv, kg.at[inner], kssem.at[d - 1], krsem.at[inner], other(d)))

    def arrived(b):
        pltpu.make_async_remote_copy(
            src_ref=q, dst_ref=qa.at[b], send_sem=ssem.at[0], recv_sem=rsem.at[b],
            device_id={"seq": other(1)}, device_id_type=MESH).wait_recv()

    for e in range(1, n_req):
        b = across(n_req - e)
        arrived(b)
        for d in range(1, group):
            sent.append(send(qa.at[b], qa.at[b], fsem.at[(e - 1) * (group - 1) + d - 1],
                             rsem.at[b], other(d)))
    for d in range(1, group):
        arrived(other(d))
        m = mate(d)
        pltpu.make_async_remote_copy(
            src_ref=kv, dst_ref=kg.at[m], send_sem=kssem.at[0], recv_sem=krsem.at[m],
            device_id={"seq": other(1)}, device_id_type=MESH).wait_recv()
        for e in range(1, n_req):
            arrived(lax.rem(grp + e, n_req) * group + m)
    for c in sent:
        c.wait_send()
    own_q.wait()
    own_kv.wait()


def page_kernel(page_table, cache_len, first, qa, pool, acc_out, stat_out,
                kbuf, vbuf, m_ref, l_ref, acc, owner, limit, ksem, vsem):
    n_slots, page_len, width = kbuf.shape
    heads = width // HD
    n_req, n_pages = page_table.shape
    for s in range(n_slots):
        pltpu.make_async_copy(pool.at[0, s], kbuf.at[s], ksem.at[s]).start()
        pltpu.make_async_copy(pool.at[1, s], vbuf.at[s], vsem.at[s]).start()
    m_ref[...] = jnp.full(m_ref.shape, NEGATIVE, jnp.float32)
    l_ref[...] = jnp.zeros(l_ref.shape, jnp.float32)
    acc[...] = jnp.zeros(acc.shape, jnp.float32)
    for s in range(n_slots):
        owner[s] = 0
        limit[s] = 0
    base = first[0]
    for r in range(n_req):
        length = cache_len[r]
        for j in range(n_pages):
            slot = page_table[r, j] - base

            @pl.when((page_table[r, j] >= 0) & (slot >= 0) & (slot < n_slots))
            def _():
                owner[slot] = r
                limit[slot] = length - j * page_len

    scale = 1.0 / math.sqrt(HD)

    def step(s, carry):
        pltpu.make_async_copy(pool.at[0, s], kbuf.at[s], ksem.at[s]).wait()
        pltpu.make_async_copy(pool.at[1, s], vbuf.at[s], vsem.at[s]).wait()
        left = limit[s]

        @pl.when(left > 0)
        def _():
            r = owner[s]
            scores = []
            for h in range(heads):
                cols = slice(h * HD, (h + 1) * HD)
                scores.append(lax.dot_general(
                    qa[r, :, cols], kbuf[s, :, cols], NT, preferred_element_type=jnp.float32))
            live = lax.broadcasted_iota(jnp.int32, scores[0].shape, 1) < left
            probs = []
            scales = []
            for h in range(heads):
                x = jnp.where(live, scores[h] * scale, NEGATIVE)
                old = m_ref[r, h]
                new = jnp.maximum(old, jnp.max(x, axis=1, keepdims=True))
                p = jnp.exp(x - new)
                a = jnp.exp(old - new)
                m_ref[r, h] = new
                l_ref[r, h] = a * l_ref[r, h] + jnp.sum(p, axis=1, keepdims=True)
                probs.append(p.astype(jnp.bfloat16))
                scales.append(a)
            for h in range(heads):
                cols = slice(h * HD, (h + 1) * HD)
                o = jnp.dot(probs[h], vbuf[s, :, cols], preferred_element_type=jnp.float32)
                acc[r, :, cols] = scales[h] * acc[r, :, cols] + o

        return carry

    lax.fori_loop(0, n_slots, step, 0)
    acc_out[...] = acc[...].astype(jnp.bfloat16)
    n_draft = acc.shape[1]
    lane = lax.broadcasted_iota(jnp.int32, (n_draft, HD), 1)
    for r in range(n_req):
        stat = jnp.zeros((n_draft, HD), jnp.float32)
        for h in range(heads):
            stat = jnp.where(lane == h, m_ref[r, h], stat)
            stat = jnp.where(lane == HD // 2 + h, l_ref[r, h], stat)
        stat_out[r] = stat


def finish_kernel(n_seq, n_tp, group, q, kg, mask, part, stat, weight, out,
                  got, gstat, wbuf, att, tree, pbuf, prbuf,
                  asem, arsem, tsem, trsem, wsem, psem, prsem, lsem):
    me = lax.axis_index("seq")
    tp = lax.axis_index("tp")
    rows, width = q.shape
    heads = width // HD
    out_w = out.shape[1]
    barrier = pltpu.get_barrier_semaphore()
    for d in range(1, n_seq):
        pl.semaphore_signal(barrier, inc=1, device_id={"seq": lax.rem(me + d, n_seq)},
                            device_id_type=MESH)
    for d in range(1, n_tp):
        pl.semaphore_signal(barrier, inc=1, device_id={"tp": lax.rem(tp + d, n_tp)},
                            device_id_type=MESH)
    own_part = pltpu.make_async_copy(part.at[me], got.at[me], lsem.at[0])
    own_stat = pltpu.make_async_copy(stat.at[me], gstat.at[me], lsem.at[1])
    own_part.start()
    own_stat.start()
    loads = []
    for t in range(n_tp):
        c = pltpu.make_async_copy(weight.at[:, pl.ds(t * out_w, out_w)], wbuf.at[t], wsem.at[t])
        c.start()
        loads.append(c)
    pl.semaphore_wait(barrier, n_seq + n_tp - 2)
    sent = []
    for d in range(1, n_seq):
        peer = lax.rem(me + d, n_seq)
        for src, dst, s, r in ((stat, gstat, tsem, trsem), (part, got, asem, arsem)):
            c = pltpu.make_async_remote_copy(
                src_ref=src.at[peer], dst_ref=dst.at[me], send_sem=s.at[d - 1],
                recv_sem=r.at[me], device_id={"seq": peer}, device_id_type=MESH)
            c.start()
            sent.append(c)

    scale = 1.0 / math.sqrt(HD)
    allowed = mask[me] == 1
    tree_m = []
    tree_l = []
    for h in range(heads):
        cols = slice(h * HD, (h + 1) * HD)
        keys = jnp.concatenate([kg[g, 0, :, cols] for g in range(group)], axis=0)
        values = jnp.concatenate([kg[g, 1, :, cols] for g in range(group)], axis=0)
        x = lax.dot_general(q[:, cols], keys, NT, preferred_element_type=jnp.float32) * scale
        x = jnp.where(allowed, x, NEGATIVE)
        top = jnp.max(x, axis=1, keepdims=True)
        p = jnp.where(allowed, jnp.exp(x - top), 0.0)
        tree_m.append(top)
        tree_l.append(jnp.sum(p, axis=1, keepdims=True))
        tree[:, cols] = jnp.dot(p.astype(jnp.bfloat16), values, preferred_element_type=jnp.float32)

    own_part.wait()
    own_stat.wait()
    for d in range(1, n_seq):
        src = lax.rem(me + n_seq - d, n_seq)
        for a, b, s, r in ((stat, gstat, tsem, trsem), (part, got, asem, arsem)):
            pltpu.make_async_remote_copy(
                src_ref=a.at[src], dst_ref=b.at[src], send_sem=s.at[d - 1],
                recv_sem=r.at[src], device_id={"seq": src}, device_id_type=MESH).wait_recv()
    for h in range(heads):
        cols = slice(h * HD, (h + 1) * HD)
        top = tree_m[h]
        for i in range(n_seq):
            top = jnp.maximum(top, gstat[i, :, h:h + 1])
        f = jnp.exp(tree_m[h] - top)
        den = f * tree_l[h]
        num = f * tree[:, cols]
        for i in range(n_seq):
            f = jnp.exp(gstat[i, :, h:h + 1] - top)
            den = den + f * gstat[i, :, HD // 2 + h:HD // 2 + h + 1]
            num = num + f * got[i, :, cols].astype(jnp.float32)
        att[:, cols] = (num / den).astype(jnp.bfloat16)
    for c in loads:
        c.wait()
    for d in range(1, n_tp):
        peer = lax.rem(tp + d, n_tp)
        pbuf[d - 1] = jnp.dot(att[...], wbuf[peer],
                              preferred_element_type=jnp.float32).astype(jnp.bfloat16)
        c = pltpu.make_async_remote_copy(
            src_ref=pbuf.at[d - 1], dst_ref=prbuf.at[d - 1], send_sem=psem.at[d - 1],
            recv_sem=prsem.at[d - 1], device_id={"tp": peer}, device_id_type=MESH)
        c.start()
        sent.append(c)
    total = jnp.dot(att[...], wbuf[tp], preferred_element_type=jnp.float32)
    for d in range(1, n_tp):
        pltpu.make_async_remote_copy(
            src_ref=pbuf.at[d - 1], dst_ref=prbuf.at[d - 1], send_sem=psem.at[d - 1],
            recv_sem=prsem.at[d - 1], device_id={"tp": lax.rem(tp + d, n_tp)},
            device_id_type=MESH).wait_recv()
        total = total + prbuf[d - 1].astype(jnp.float32)
    out[...] = total.astype(out.dtype)
    for c in sent:
        c.wait_send()


def body(draft_q, draft_kv, kv_pool, page_table, cache_len, tree_mask, accepted_rows, out_weight):
    n_seq = lax.axis_size("seq")
    n_tp = lax.axis_size("tp")
    rows, width = draft_q.shape
    heads = width // HD
    n_req, n_pages = page_table.shape
    n_draft = tree_mask.shape[1]
    n_slots, page_len = kv_pool.shape[1:3]
    group = n_seq // n_req
    out_w = out_weight.shape[1] // n_tp
    bf16, f32 = jnp.bfloat16, jnp.float32
    dma = pltpu.SemaphoreType.DMA

    query_all, group_kv = pl.pallas_call(
        functools.partial(gather_kernel, n_req, group),
        out_shape=(jax.ShapeDtypeStruct((n_seq, rows, width), bf16),
                   jax.ShapeDtypeStruct((group, 2, rows, width), bf16)),
        in_specs=[ANY, ANY],
        out_specs=(ANY, ANY),
        scratch_shapes=[dma((n_req + group - 2,)), dma((n_seq,)),
                        dma(((n_req - 1) * (group - 1),)), dma((group - 1,)), dma((group,)),
                        dma((2,))],
        compiler_params=pltpu.CompilerParams(collective_id=0, has_side_effects=True),
    )(draft_q, draft_kv)

    first = (lax.axis_index("seq") * n_slots).astype(jnp.int32).reshape(1)
    part, stat = pl.pallas_call(
        page_kernel,
        out_shape=(jax.ShapeDtypeStruct((n_req, n_draft, width), bf16),
                   jax.ShapeDtypeStruct((n_req, n_draft, HD), f32)),
        in_specs=[SMEM, SMEM, SMEM, VMEM, ANY],
        out_specs=(VMEM, VMEM),
        scratch_shapes=[pltpu.VMEM((n_slots, page_len, width), bf16),
                        pltpu.VMEM((n_slots, page_len, width), bf16),
                        pltpu.VMEM((n_req, heads, n_draft, HD), f32),
                        pltpu.VMEM((n_req, heads, n_draft, HD), f32),
                        pltpu.VMEM((n_req, n_draft, width), f32),
                        pltpu.SMEM((n_slots,), jnp.int32),
                        pltpu.SMEM((n_slots,), jnp.int32),
                        dma((n_slots,)), dma((n_slots,))],
        compiler_params=pltpu.CompilerParams(vmem_limit_bytes=32 << 20),
        cost_estimate=pl.CostEstimate(flops=10 ** 10, bytes_accessed=3 * 10 ** 7,
                                      transcendentals=10 ** 6),
    )(page_table, cache_len, first, query_all.reshape(n_req, n_draft, width), kv_pool)

    layer_out = pl.pallas_call(
        functools.partial(finish_kernel, n_seq, n_tp, group),
        out_shape=jax.ShapeDtypeStruct((rows, out_w), bf16),
        in_specs=[VMEM, VMEM, VMEM, ANY, ANY, ANY],
        out_specs=VMEM,
        scratch_shapes=[pltpu.VMEM((n_seq, rows, width), bf16),
                        pltpu.VMEM((n_seq, rows, HD), f32),
                        pltpu.VMEM((n_tp, width, out_w), bf16),
                        pltpu.VMEM((rows, width), bf16),
                        pltpu.VMEM((rows, width), f32),
                        pltpu.VMEM((n_tp - 1, rows, out_w), bf16),
                        pltpu.VMEM((n_tp - 1, rows, out_w), bf16),
                        dma((n_seq - 1,)), dma((n_seq,)), dma((n_seq - 1,)), dma((n_seq,)),
                        dma((n_tp,)), dma((n_tp - 1,)), dma((n_tp - 1,)), dma((2,))],
        compiler_params=pltpu.CompilerParams(collective_id=1, has_side_effects=True,
                                             vmem_limit_bytes=32 << 20),
        cost_estimate=pl.CostEstimate(flops=10 ** 10, bytes_accessed=3 * 10 ** 7,
                                      transcendentals=10 ** 6),
    )(draft_q, group_kv, tree_mask.reshape(n_seq, rows, n_draft),
      part.reshape(n_seq, rows, width), stat.reshape(n_seq, rows, HD), out_weight)

    kv_all = lax.all_gather(draft_kv, "seq", axis=1, tiled=True)
    picked = jnp.concatenate(
        [accepted_rows, jnp.full((n_req, page_len - n_draft), -1, jnp.int32)], axis=1)
    onehot = (picked[:, :, None] == jnp.arange(n_draft, dtype=jnp.int32)[None, None, :]).astype(bf16)
    accepted_kv = jnp.einsum(
        "rji,crid->crjd", onehot, kv_all.reshape(2, n_req, n_draft, width),
        preferred_element_type=f32).astype(bf16)
    return (layer_out, accepted_kv)


def solution(mesh):
    return jax.shard_map(
        body,
        mesh=mesh,
        in_specs=(P("seq", "tp"), P(None, "seq", "tp"), P(None, "seq", None, "tp"),
                  P(), P(), P(), P(), P("tp", None)),
        out_specs=(P("seq", "tp"), P(None, None, None, "tp")),
        check_vma=False,
    )
```

```python
import functools
import math

import jax
import jax.numpy as jnp
from jax import lax
from jax.experimental import pallas as pl
from jax.experimental.pallas import tpu as pltpu
from jax.sharding import PartitionSpec as P

HD = 128
NEGATIVE = -1e30
MESH = pl.DeviceIdType.MESH
ANY = pl.BlockSpec(memory_space=pl.ANY)
VMEM = pl.BlockSpec(memory_space=pltpu.VMEM)
SMEM = pl.BlockSpec(memory_space=pltpu.SMEM)
NT = (((1,), (1,)), ((), ()))


def fused_kernel(n_req, n_pages, n_seq, n_tp, group, code, cache_len, mask, q, kv, pool, weight,
                 out, kva,
                 qa, kbuf, vbuf, m_st, l_st, acc_st, part, stat, got, gstat, kg, wbuf, att, tree,
                 pbuf, prbuf, last,
                 qsem, qrsem, fsem, cssem, crsem, cfsem, lsem, ksem, vsem, gsem,
                 asem, arsem, tsem, trsem, wsem, psem, prsem):
    me = lax.axis_index("seq")
    tp = lax.axis_index("tp")
    grp = me // group
    inner = lax.rem(me, group)
    n_slots, page_len, width = kbuf.shape
    rows = qa.shape[1] // group
    n_draft = qa.shape[1]
    heads = width // HD
    out_w = out.shape[1]
    scale = 1.0 / math.sqrt(HD)

    def across(d):
        return lax.rem(grp + d, n_req) * group + inner

    def other(d):
        return grp * group + lax.rem(inner + d, group)

    def remote(a, b, s, r, where):
        return pltpu.make_async_remote_copy(
            src_ref=a, dst_ref=b, send_sem=s, recv_sem=r, device_id=where, device_id_type=MESH)

    def block(i):
        return qa.at[i // group, pl.ds(pl.multiple_of(lax.rem(i, group) * rows, rows), rows)]

    barrier = pltpu.get_barrier_semaphore()
    for d in range(1, n_seq):
        pl.semaphore_signal(barrier, inc=1, device_id={"seq": lax.rem(me + d, n_seq)},
                            device_id_type=MESH)
    for d in range(1, n_tp):
        pl.semaphore_signal(barrier, inc=1, device_id={"tp": lax.rem(tp + d, n_tp)},
                            device_id_type=MESH)
    own_q = pltpu.make_async_copy(q, block(me), lsem.at[0])
    own_q.start()
    own_kv = pltpu.make_async_copy(kv, kva.at[me], lsem.at[1])
    own_kv.start()
    for s in range(n_slots):
        pltpu.make_async_copy(pool.at[0, s], kbuf.at[s], ksem.at[s]).start()
        pltpu.make_async_copy(pool.at[1, s], vbuf.at[s], vsem.at[s]).start()
    loads = []
    for t in range(n_tp):
        c = pltpu.make_async_copy(weight.at[:, pl.ds(t * out_w, out_w)], wbuf.at[t], wsem.at[t])
        c.start()
        loads.append(c)
    m_st[0] = jnp.full(m_st.shape[1:], NEGATIVE, jnp.float32)
    l_st[0] = jnp.zeros(l_st.shape[1:], jnp.float32)
    acc_st[0] = jnp.zeros(acc_st.shape[1:], jnp.float32)
    for r in range(n_req):
        last[r] = 0
    pl.semaphore_wait(barrier, n_seq + n_tp - 2)

    sent = []

    def send(*args):
        c = remote(*args)
        c.start()
        sent.append(c)

    for d in range(n_req - 1, 0, -1):
        send(q, block(me), qsem.at[d - 1], qrsem.at[me], {"seq": across(d)})
    for d in range(1, group):
        send(q, block(me), qsem.at[n_req - 2 + d], qrsem.at[me], {"seq": other(d)})
    for d in range(1, group):
        send(kv, kva.at[me], cssem.at[n_req - 2 + d], crsem.at[me], {"seq": other(d)})
    for d in range(n_req - 1, 0, -1):
        send(kv, kva.at[me], cssem.at[d - 1], crsem.at[me], {"seq": across(d)})

    def q_arrived(b):
        remote(q, block(b), qsem.at[0], qrsem.at[b], {"seq": other(1)}).wait_recv()

    def kv_arrived(b):
        remote(kv, kva.at[b], cssem.at[0], crsem.at[b], {"seq": other(1)}).wait_recv()

    for e in range(1, n_req):
        b = across(e)
        q_arrived(b)
        for d in range(1, group):
            send(block(b), block(b), fsem.at[(e - 1) * (group - 1) + d - 1], qrsem.at[b],
                 {"seq": other(d)})
    for d in range(1, group):
        q_arrived(other(d))
        for e in range(1, n_req):
            q_arrived(lax.rem(grp + e, n_req) * group + lax.rem(inner + d, group))
    own_q.wait()

    def forward(e, d, start):
        b = across(e)
        c = remote(kva.at[b], kva.at[b], cfsem.at[(e - 1) * (group - 1) + d - 1], crsem.at[b],
                   {"seq": other(d)})
        if start:
            c.start()
        else:
            c.wait_send()

    def step(s, carry):
        pltpu.make_async_copy(pool.at[0, s], kbuf.at[s], ksem.at[s]).wait()
        pltpu.make_async_copy(pool.at[1, s], vbuf.at[s], vsem.at[s]).wait()
        number = code[s]
        place = jnp.maximum(number - 1, 0)
        r = lax.div(place, n_pages)
        left = jnp.where(number > 0, cache_len[r] - (place - r * n_pages) * page_len, 0)
        prev = last[r]
        scores = []
        for h in range(heads):
            cols = slice(h * HD, (h + 1) * HD)
            scores.append(lax.dot_general(
                qa[r, :, cols], kbuf[s, :, cols], NT, preferred_element_type=jnp.float32))
        live = lax.broadcasted_iota(jnp.int32, scores[0].shape, 1) < left
        probs = []
        scales = []
        for h in range(heads):
            x = jnp.where(live, scores[h] * scale, NEGATIVE)
            old = m_st[prev, h]
            new = jnp.maximum(old, jnp.max(x, axis=1, keepdims=True))
            p = jnp.exp(x - new)
            a = jnp.exp(old - new)
            m_st[s + 1, h] = new
            l_st[s + 1, h] = a * l_st[prev, h] + jnp.sum(p, axis=1, keepdims=True)
            probs.append(p.astype(jnp.bfloat16))
            scales.append(a)
        for h in range(heads):
            cols = slice(h * HD, (h + 1) * HD)
            o = jnp.dot(probs[h], vbuf[s, :, cols], preferred_element_type=jnp.float32)
            acc_st[s + 1, :, cols] = scales[h] * acc_st[prev, :, cols] + o
        for i in range(n_req):
            last[i] = jnp.where((left > 0) & (r == i), s + 1, last[i])
        return carry

    cuts = [n_slots * e // n_req for e in range(n_req + 1)]
    for e in range(n_req):
        lax.fori_loop(cuts[e], cuts[e + 1], step, 0)
        if e + 1 < n_req:
            kv_arrived(across(e + 1))
            for d in range(1, group):
                forward(e + 1, d, True)

    lane = lax.broadcasted_iota(jnp.int32, (n_draft, HD), 1)
    for r in range(n_req):
        at = last[r]
        acc = acc_st[at].astype(jnp.bfloat16)
        info = jnp.zeros((n_draft, HD), jnp.float32)
        for h in range(heads):
            info = jnp.where(lane == h, m_st[at, h], info)
            info = jnp.where(lane == HD // 2 + h, l_st[at, h], info)
        for g in range(group):
            part[r * group + g] = acc[g * rows:(g + 1) * rows]
            stat[r * group + g] = info[g * rows:(g + 1) * rows]
    own_part = pltpu.make_async_copy(part.at[me], got.at[me], lsem.at[2])
    own_stat = pltpu.make_async_copy(stat.at[me], gstat.at[me], lsem.at[3])
    own_part.start()
    own_stat.start()
    for d in range(1, n_seq):
        peer = lax.rem(me + d, n_seq)
        send(stat.at[peer], gstat.at[me], tsem.at[d - 1], trsem.at[me], {"seq": peer})
        send(part.at[peer], got.at[me], asem.at[d - 1], arsem.at[me], {"seq": peer})

    own_kv.wait()
    for d in range(1, group):
        kv_arrived(other(d))
    tree_in = []
    for g in range(group):
        c = pltpu.make_async_copy(kva.at[grp * group + g], kg.at[g], gsem.at[g])
        c.start()
        tree_in.append(c)
    for c in tree_in:
        c.wait()
    allowed = mask[me] == 1
    mine = qa[grp, pl.ds(pl.multiple_of(inner * rows, rows), rows), :]
    tree_m = []
    tree_l = []
    for h in range(heads):
        cols = slice(h * HD, (h + 1) * HD)
        keys = jnp.concatenate([kg[g, 0, :, cols] for g in range(group)], axis=0)
        values = jnp.concatenate([kg[g, 1, :, cols] for g in range(group)], axis=0)
        x = lax.dot_general(mine[:, cols], keys, NT, preferred_element_type=jnp.float32) * scale
        x = jnp.where(allowed, x, NEGATIVE)
        top = jnp.max(x, axis=1, keepdims=True)
        p = jnp.where(allowed, jnp.exp(x - top), 0.0)
        tree_m.append(top)
        tree_l.append(jnp.sum(p, axis=1, keepdims=True))
        tree[:, cols] = jnp.dot(p.astype(jnp.bfloat16), values, preferred_element_type=jnp.float32)

    own_part.wait()
    own_stat.wait()
    for d in range(1, n_seq):
        i = lax.rem(me + n_seq - d, n_seq)
        remote(stat.at[i], gstat.at[i], tsem.at[d - 1], trsem.at[i], {"seq": i}).wait_recv()
        remote(part.at[i], got.at[i], asem.at[d - 1], arsem.at[i], {"seq": i}).wait_recv()
    for h in range(heads):
        cols = slice(h * HD, (h + 1) * HD)
        top = tree_m[h]
        for i in range(n_seq):
            top = jnp.maximum(top, gstat[i, :, h:h + 1])
        f = jnp.exp(tree_m[h] - top)
        den = f * tree_l[h]
        num = f * tree[:, cols]
        for i in range(n_seq):
            f = jnp.exp(gstat[i, :, h:h + 1] - top)
            den = den + f * gstat[i, :, HD // 2 + h:HD // 2 + h + 1]
            num = num + f * got[i, :, cols].astype(jnp.float32)
        att[:, cols] = (num / den).astype(jnp.bfloat16)
    for c in loads:
        c.wait()
    for d in range(1, n_tp):
        peer = lax.rem(tp + d, n_tp)
        pbuf[d - 1] = jnp.dot(att[...], wbuf[peer],
                              preferred_element_type=jnp.float32).astype(jnp.bfloat16)
        c = pltpu.make_async_remote_copy(
            src_ref=pbuf.at[d - 1], dst_ref=prbuf.at[d - 1], send_sem=psem.at[d - 1],
            recv_sem=prsem.at[d - 1], device_id={"tp": peer}, device_id_type=MESH)
        c.start()
        sent.append(c)
    total = jnp.dot(att[...], wbuf[tp], preferred_element_type=jnp.float32)
    for d in range(1, n_tp):
        pltpu.make_async_remote_copy(
            src_ref=pbuf.at[d - 1], dst_ref=prbuf.at[d - 1], send_sem=psem.at[d - 1],
            recv_sem=prsem.at[d - 1], device_id={"tp": lax.rem(tp + d, n_tp)},
            device_id_type=MESH).wait_recv()
        total = total + prbuf[d - 1].astype(jnp.float32)
    out[...] = total.astype(out.dtype)
    for d in range(1, group):
        for e in range(1, n_req):
            kv_arrived(lax.rem(grp + e, n_req) * group + lax.rem(inner + d, group))
    for e in range(1, n_req):
        for d in range(1, group):
            forward(e, d, False)
    for c in sent:
        c.wait_send()


def accept_kernel(rows_ref, kv, out):
    group, rows, width = kv.shape[1], kv.shape[3], kv.shape[4]
    n_draft = group * rows
    pick = lax.broadcasted_iota(jnp.int32, (n_draft, n_draft), 0) == rows_ref[0]
    blocks = jnp.concatenate([kv[0, g, 0] for g in range(group)], axis=0)
    out[0, 0, :n_draft] = lax.dot_general(
        pick.astype(jnp.bfloat16), blocks, (((0,), (0,)), ((), ())),
        preferred_element_type=jnp.float32).astype(out.dtype)
    out[0, 0, n_draft:] = jnp.zeros((out.shape[2] - n_draft, width), out.dtype)


def body(draft_q, draft_kv, kv_pool, page_table, cache_len, tree_mask, accepted_rows, out_weight):
    n_seq = lax.axis_size("seq")
    n_tp = lax.axis_size("tp")
    rows, width = draft_q.shape
    heads = width // HD
    n_req, n_pages = page_table.shape
    n_draft = tree_mask.shape[1]
    n_slots, page_len = kv_pool.shape[1:3]
    group = n_seq // n_req
    out_w = out_weight.shape[1] // n_tp
    bf16, f32 = jnp.bfloat16, jnp.float32
    dma = pltpu.SemaphoreType.DMA

    slots = lax.axis_index("seq") * n_slots + jnp.arange(n_slots, dtype=jnp.int32)
    number = jnp.arange(1, n_req * n_pages + 1, dtype=jnp.int32)
    code = jnp.sum(jnp.where(page_table.reshape(1, -1) == slots[:, None], number[None], 0), axis=1)

    layer_out, kv_all = pl.pallas_call(
        functools.partial(fused_kernel, n_req, n_pages, n_seq, n_tp, group),
        out_shape=(jax.ShapeDtypeStruct((rows, out_w), bf16),
                   jax.ShapeDtypeStruct((n_seq, 2, rows, width), bf16)),
        in_specs=[SMEM, SMEM, VMEM, ANY, ANY, ANY, ANY],
        out_specs=(VMEM, ANY),
        scratch_shapes=[pltpu.VMEM((n_req, n_draft, width), bf16),
                        pltpu.VMEM((n_slots, page_len, width), bf16),
                        pltpu.VMEM((n_slots, page_len, width), bf16),
                        pltpu.VMEM((n_slots + 1, heads, n_draft, HD), f32),
                        pltpu.VMEM((n_slots + 1, heads, n_draft, HD), f32),
                        pltpu.VMEM((n_slots + 1, n_draft, width), f32),
                        pltpu.VMEM((n_seq, rows, width), bf16),
                        pltpu.VMEM((n_seq, rows, HD), f32),
                        pltpu.VMEM((n_seq, rows, width), bf16),
                        pltpu.VMEM((n_seq, rows, HD), f32),
                        pltpu.VMEM((group, 2, rows, width), bf16),
                        pltpu.VMEM((n_tp, width, out_w), bf16),
                        pltpu.VMEM((rows, width), bf16),
                        pltpu.VMEM((rows, width), f32),
                        pltpu.VMEM((n_tp - 1, rows, out_w), bf16),
                        pltpu.VMEM((n_tp - 1, rows, out_w), bf16),
                        pltpu.SMEM((n_req,), jnp.int32),
                        dma((n_req + group - 2,)), dma((n_seq,)),
                        dma(((n_req - 1) * (group - 1),)),
                        dma((n_req + group - 2,)), dma((n_seq,)),
                        dma(((n_req - 1) * (group - 1),)),
                        dma((4,)), dma((n_slots,)), dma((n_slots,)), dma((group,)),
                        dma((n_seq - 1,)), dma((n_seq,)), dma((n_seq - 1,)), dma((n_seq,)),
                        dma((n_tp,)), dma((n_tp - 1,)), dma((n_tp - 1,))],
        compiler_params=pltpu.CompilerParams(collective_id=0, has_side_effects=True,
                                             vmem_limit_bytes=58 << 20),
        cost_estimate=pl.CostEstimate(flops=10 ** 10, bytes_accessed=3 * 10 ** 7,
                                      transcendentals=10 ** 6),
    )(code, cache_len, tree_mask.reshape(n_seq, rows, n_draft), draft_q, draft_kv, kv_pool,
      out_weight)

    accepted_kv = pl.pallas_call(
        accept_kernel,
        grid=(n_req, 2),
        out_shape=jax.ShapeDtypeStruct((2, n_req, page_len, width), bf16),
        in_specs=[pl.BlockSpec((1, 1, n_draft), lambda r, c: (r, 0, 0)),
                  pl.BlockSpec((1, group, 1, rows, width), lambda r, c: (r, 0, c, 0, 0))],
        out_specs=pl.BlockSpec((1, 1, page_len, width), lambda r, c: (c, r, 0, 0)),
    )(accepted_rows.reshape(n_req, 1, n_draft), kv_all.reshape(n_req, group, 2, rows, width))
    return (layer_out, accepted_kv)


def solution(mesh):
    return jax.shard_map(
        body,
        mesh=mesh,
        in_specs=(P("seq", "tp"), P(None, "seq", "tp"), P(None, "seq", None, "tp"),
                  P(), P(), P(), P(), P("tp", None)),
        out_specs=(P("seq", "tp"), P(None, None, None, "tp")),
        check_vma=False,
    )
```

```python
import functools
import math

import jax
import jax.numpy as jnp
from jax import lax
from jax.experimental import pallas as pl
from jax.experimental.pallas import tpu as pltpu
from jax.sharding import PartitionSpec as P

HD = 128
NEGATIVE = -1e30
MESH = pl.DeviceIdType.MESH
ANY = pl.BlockSpec(memory_space=pl.ANY)
VMEM = pl.BlockSpec(memory_space=pltpu.VMEM)
SMEM = pl.BlockSpec(memory_space=pltpu.SMEM)
NT = (((1,), (1,)), ((), ()))


def fused_kernel(n_req, n_pages, n_seq, n_tp, group, table, cache_len, mask, q, kv, pool, weight,
                 out, kva,
                 qa, kbuf, vbuf, m_st, l_st, acc_st, part, stat, got, gstat, kg, wbuf, att, tree,
                 pbuf, prbuf, last, code,
                 qsem, qrsem, fsem, cssem, crsem, cfsem, lsem, ksem, vsem, gsem,
                 asem, arsem, tsem, trsem, wsem, psem, prsem):
    me = lax.axis_index("seq")
    tp = lax.axis_index("tp")
    grp = me // group
    inner = lax.rem(me, group)
    n_slots, page_len, width = kbuf.shape
    rows = qa.shape[1] // group
    n_draft = qa.shape[1]
    heads = width // HD
    out_w = out.shape[1]
    scale = 1.0 / math.sqrt(HD)

    def across(d):
        return lax.rem(grp + d, n_req) * group + inner

    def other(d):
        return grp * group + lax.rem(inner + d, group)

    def remote(a, b, s, r, where):
        return pltpu.make_async_remote_copy(
            src_ref=a, dst_ref=b, send_sem=s, recv_sem=r, device_id=where, device_id_type=MESH)

    def block(i):
        return qa.at[i // group, pl.ds(pl.multiple_of(lax.rem(i, group) * rows, rows), rows)]

    barrier = pltpu.get_barrier_semaphore()
    for d in range(1, n_seq):
        pl.semaphore_signal(barrier, inc=1, device_id={"seq": lax.rem(me + d, n_seq)},
                            device_id_type=MESH)
    for d in range(1, n_tp):
        pl.semaphore_signal(barrier, inc=1, device_id={"tp": lax.rem(tp + d, n_tp)},
                            device_id_type=MESH)
    own_q = pltpu.make_async_copy(q, block(me), lsem.at[0])
    own_q.start()
    own_kv = pltpu.make_async_copy(kv, kva.at[me], lsem.at[1])
    own_kv.start()
    m_st[0] = jnp.full(m_st.shape[1:], NEGATIVE, jnp.float32)
    l_st[0] = jnp.zeros(l_st.shape[1:], jnp.float32)
    acc_st[0] = jnp.zeros(acc_st.shape[1:], jnp.float32)
    for r in range(n_req):
        last[r] = 0
    pl.semaphore_wait(barrier, n_seq + n_tp - 2)

    sent = []

    def send(*args):
        c = remote(*args)
        c.start()
        sent.append(c)

    for d in range(n_req - 1, 0, -1):
        send(q, block(me), qsem.at[d - 1], qrsem.at[me], {"seq": across(d)})
    for d in range(1, group):
        send(q, block(me), qsem.at[n_req - 2 + d], qrsem.at[me], {"seq": other(d)})
    for d in range(1, group):
        send(kv, kva.at[me], cssem.at[n_req - 2 + d], crsem.at[me], {"seq": other(d)})
    for d in range(n_req - 1, 0, -1):
        send(kv, kva.at[me], cssem.at[d - 1], crsem.at[me], {"seq": across(d)})

    def q_arrived(b):
        remote(q, block(b), qsem.at[0], qrsem.at[b], {"seq": other(1)}).wait_recv()

    def kv_arrived(b):
        remote(kv, kva.at[b], cssem.at[0], crsem.at[b], {"seq": other(1)}).wait_recv()

    for s in range(n_slots):
        pltpu.make_async_copy(pool.at[0, s], kbuf.at[s], ksem.at[s]).start()
        pltpu.make_async_copy(pool.at[1, s], vbuf.at[s], vsem.at[s]).start()
    loads = []
    for t in range(n_tp):
        c = pltpu.make_async_copy(weight.at[:, pl.ds(t * out_w, out_w)], wbuf.at[t], wsem.at[t])
        c.start()
        loads.append(c)
    shape = table.shape
    number = (lax.broadcasted_iota(jnp.int32, shape, 0) * n_pages
              + lax.broadcasted_iota(jnp.int32, shape, 1) + 1)
    for s in range(n_slots):
        code[s] = jnp.sum(jnp.where(table[...] == me * n_slots + s, number, 0))

    for e in range(1, n_req):
        b = across(e)
        q_arrived(b)
        for d in range(1, group):
            send(block(b), block(b), fsem.at[(e - 1) * (group - 1) + d - 1], qrsem.at[b],
                 {"seq": other(d)})
    for d in range(1, group):
        q_arrived(other(d))
        for e in range(1, n_req):
            q_arrived(lax.rem(grp + e, n_req) * group + lax.rem(inner + d, group))
    own_q.wait()

    def forward(e, d, start):
        b = across(e)
        c = remote(kva.at[b], kva.at[b], cfsem.at[(e - 1) * (group - 1) + d - 1], crsem.at[b],
                   {"seq": other(d)})
        if start:
            c.start()
        else:
            c.wait_send()

    def step(s, carry):
        pltpu.make_async_copy(pool.at[0, s], kbuf.at[s], ksem.at[s]).wait()
        pltpu.make_async_copy(pool.at[1, s], vbuf.at[s], vsem.at[s]).wait()
        number = code[s]
        place = jnp.maximum(number - 1, 0)
        r = jnp.minimum(lax.div(place, n_pages), n_req - 1)
        left = jnp.where(number > 0, cache_len[r] - (place - r * n_pages) * page_len, 0)
        prev = last[r]
        scores = []
        for h in range(heads):
            cols = slice(h * HD, (h + 1) * HD)
            scores.append(lax.dot_general(
                qa[r, :, cols], kbuf[s, :, cols], NT, preferred_element_type=jnp.float32))
        live = lax.broadcasted_iota(jnp.int32, scores[0].shape, 1) < left
        probs = []
        scales = []
        for h in range(heads):
            x = jnp.where(live, scores[h] * scale, NEGATIVE)
            old = m_st[prev, h]
            new = jnp.maximum(old, jnp.max(x, axis=1, keepdims=True))
            p = jnp.exp(x - new)
            a = jnp.exp(old - new)
            m_st[s + 1, h] = new
            l_st[s + 1, h] = a * l_st[prev, h] + jnp.sum(p, axis=1, keepdims=True)
            probs.append(p.astype(jnp.bfloat16))
            scales.append(a)
        for h in range(heads):
            cols = slice(h * HD, (h + 1) * HD)
            o = jnp.dot(probs[h], vbuf[s, :, cols], preferred_element_type=jnp.float32)
            acc_st[s + 1, :, cols] = scales[h] * acc_st[prev, :, cols] + o
        for i in range(n_req):
            last[i] = jnp.where((left > 0) & (r == i), s + 1, last[i])
        return carry

    lax.fori_loop(0, n_slots, step, 0)

    lane = lax.broadcasted_iota(jnp.int32, (n_draft, HD), 1)
    for r in range(n_req):
        at = last[r]
        acc = acc_st[at].astype(jnp.bfloat16)
        info = jnp.zeros((n_draft, HD), jnp.float32)
        for h in range(heads):
            info = jnp.where(lane == h, m_st[at, h], info)
            info = jnp.where(lane == HD // 2 + h, l_st[at, h], info)
        for g in range(group):
            part[r * group + g] = acc[g * rows:(g + 1) * rows]
            stat[r * group + g] = info[g * rows:(g + 1) * rows]
    own_part = pltpu.make_async_copy(part.at[me], got.at[me], lsem.at[2])
    own_stat = pltpu.make_async_copy(stat.at[me], gstat.at[me], lsem.at[3])
    own_part.start()
    own_stat.start()
    for d in range(1, n_seq):
        peer = lax.rem(me + d, n_seq)
        send(stat.at[peer], gstat.at[me], tsem.at[d - 1], trsem.at[me], {"seq": peer})
        send(part.at[peer], got.at[me], asem.at[d - 1], arsem.at[me], {"seq": peer})

    for e in range(1, n_req):
        kv_arrived(across(e))
        for d in range(1, group):
            forward(e, d, True)

    own_kv.wait()
    for d in range(1, group):
        kv_arrived(other(d))
    tree_in = []
    for g in range(group):
        c = pltpu.make_async_copy(kva.at[grp * group + g], kg.at[g], gsem.at[g])
        c.start()
        tree_in.append(c)
    for c in tree_in:
        c.wait()
    allowed = mask[me] == 1
    mine = qa[grp, pl.ds(pl.multiple_of(inner * rows, rows), rows), :]
    tree_m = []
    tree_l = []
    for h in range(heads):
        cols = slice(h * HD, (h + 1) * HD)
        keys = jnp.concatenate([kg[g, 0, :, cols] for g in range(group)], axis=0)
        values = jnp.concatenate([kg[g, 1, :, cols] for g in range(group)], axis=0)
        x = lax.dot_general(mine[:, cols], keys, NT, preferred_element_type=jnp.float32) * scale
        x = jnp.where(allowed, x, NEGATIVE)
        top = jnp.max(x, axis=1, keepdims=True)
        p = jnp.where(allowed, jnp.exp(x - top), 0.0)
        tree_m.append(top)
        tree_l.append(jnp.sum(p, axis=1, keepdims=True))
        tree[:, cols] = jnp.dot(p.astype(jnp.bfloat16), values, preferred_element_type=jnp.float32)

    own_part.wait()
    own_stat.wait()
    for d in range(1, n_seq):
        i = lax.rem(me + n_seq - d, n_seq)
        remote(stat.at[i], gstat.at[i], tsem.at[d - 1], trsem.at[i], {"seq": i}).wait_recv()
        remote(part.at[i], got.at[i], asem.at[d - 1], arsem.at[i], {"seq": i}).wait_recv()
    for h in range(heads):
        cols = slice(h * HD, (h + 1) * HD)
        top = tree_m[h]
        for i in range(n_seq):
            top = jnp.maximum(top, gstat[i, :, h:h + 1])
        f = jnp.exp(tree_m[h] - top)
        den = f * tree_l[h]
        num = f * tree[:, cols]
        for i in range(n_seq):
            f = jnp.exp(gstat[i, :, h:h + 1] - top)
            den = den + f * gstat[i, :, HD // 2 + h:HD // 2 + h + 1]
            num = num + f * got[i, :, cols].astype(jnp.float32)
        att[:, cols] = (num / den).astype(jnp.bfloat16)
    for c in loads:
        c.wait()
    for d in range(1, n_tp):
        peer = lax.rem(tp + d, n_tp)
        pbuf[d - 1] = jnp.dot(att[...], wbuf[peer],
                              preferred_element_type=jnp.float32).astype(jnp.bfloat16)
        c = pltpu.make_async_remote_copy(
            src_ref=pbuf.at[d - 1], dst_ref=prbuf.at[d - 1], send_sem=psem.at[d - 1],
            recv_sem=prsem.at[d - 1], device_id={"tp": peer}, device_id_type=MESH)
        c.start()
        sent.append(c)
    total = jnp.dot(att[...], wbuf[tp], preferred_element_type=jnp.float32)
    for d in range(1, n_tp):
        pltpu.make_async_remote_copy(
            src_ref=pbuf.at[d - 1], dst_ref=prbuf.at[d - 1], send_sem=psem.at[d - 1],
            recv_sem=prsem.at[d - 1], device_id={"tp": lax.rem(tp + d, n_tp)},
            device_id_type=MESH).wait_recv()
        total = total + prbuf[d - 1].astype(jnp.float32)
    out[...] = total.astype(out.dtype)
    for d in range(1, group):
        for e in range(1, n_req):
            kv_arrived(lax.rem(grp + e, n_req) * group + lax.rem(inner + d, group))
    for e in range(1, n_req):
        for d in range(1, group):
            forward(e, d, False)
    for c in sent:
        c.wait_send()


def accept_kernel(rows_ref, kv, layer, out, layer_out, blocks, picked, zeros, isem, osem, zsem, lsem):
    n_req, group, _, rows, width = kv.shape
    n_draft = group * rows
    copies = []

    def copy(a, b, sem):
        c = pltpu.make_async_copy(a, b, sem)
        c.start()
        return c

    loads = []
    for r in range(n_req):
        for c in range(2):
            loads.append([copy(kv.at[r, g, c], blocks.at[r, c, pl.ds(g * rows, rows)],
                               isem.at[r, c, g]) for g in range(group)])
    copies.append(copy(layer, layer_out, lsem.at[0]))
    zeros[...] = jnp.zeros(zeros.shape, zeros.dtype)
    for r in range(n_req):
        for c in range(2):
            copies.append(copy(zeros, out.at[c, r, pl.ds(n_draft, zeros.shape[0])], zsem.at[r, c]))
    for r in range(n_req):
        pick = (lax.broadcasted_iota(jnp.int32, (n_draft, n_draft), 0)
                == rows_ref[r:r + 1, :]).astype(jnp.bfloat16)
        for c in range(2):
            for load in loads[2 * r + c]:
                load.wait()
            picked[r, c] = lax.dot_general(
                pick, blocks[r, c], (((0,), (0,)), ((), ())),
                preferred_element_type=jnp.float32).astype(out.dtype)
            copies.append(copy(picked.at[r, c], out.at[c, r, pl.ds(0, n_draft)], osem.at[r, c]))
    for c in copies:
        c.wait()


def body(draft_q, draft_kv, kv_pool, page_table, cache_len, tree_mask, accepted_rows, out_weight):
    n_seq = lax.axis_size("seq")
    n_tp = lax.axis_size("tp")
    rows, width = draft_q.shape
    heads = width // HD
    n_req, n_pages = page_table.shape
    n_draft = tree_mask.shape[1]
    n_slots, page_len = kv_pool.shape[1:3]
    group = n_seq // n_req
    out_w = out_weight.shape[1] // n_tp
    bf16, f32 = jnp.bfloat16, jnp.float32
    dma = pltpu.SemaphoreType.DMA

    layer, kv_all = pl.pallas_call(
        functools.partial(fused_kernel, n_req, n_pages, n_seq, n_tp, group),
        out_shape=(jax.ShapeDtypeStruct((rows, out_w), bf16),
                   jax.ShapeDtypeStruct((n_seq, 2, rows, width), bf16)),
        in_specs=[VMEM, SMEM, VMEM, ANY, ANY, ANY, ANY],
        out_specs=(VMEM, ANY),
        scratch_shapes=[pltpu.VMEM((n_req, n_draft, width), bf16),
                        pltpu.VMEM((n_slots, page_len, width), bf16),
                        pltpu.VMEM((n_slots, page_len, width), bf16),
                        pltpu.VMEM((n_slots + 1, heads, n_draft, HD), f32),
                        pltpu.VMEM((n_slots + 1, heads, n_draft, HD), f32),
                        pltpu.VMEM((n_slots + 1, n_draft, width), f32),
                        pltpu.VMEM((n_seq, rows, width), bf16),
                        pltpu.VMEM((n_seq, rows, HD), f32),
                        pltpu.VMEM((n_seq, rows, width), bf16),
                        pltpu.VMEM((n_seq, rows, HD), f32),
                        pltpu.VMEM((group, 2, rows, width), bf16),
                        pltpu.VMEM((n_tp, width, out_w), bf16),
                        pltpu.VMEM((rows, width), bf16),
                        pltpu.VMEM((rows, width), f32),
                        pltpu.VMEM((n_tp - 1, rows, out_w), bf16),
                        pltpu.VMEM((n_tp - 1, rows, out_w), bf16),
                        pltpu.SMEM((n_req,), jnp.int32), pltpu.SMEM((n_slots,), jnp.int32),
                        dma((n_req + group - 2,)), dma((n_seq,)),
                        dma(((n_req - 1) * (group - 1),)),
                        dma((n_req + group - 2,)), dma((n_seq,)),
                        dma(((n_req - 1) * (group - 1),)),
                        dma((4,)), dma((n_slots,)), dma((n_slots,)), dma((group,)),
                        dma((n_seq - 1,)), dma((n_seq,)), dma((n_seq - 1,)), dma((n_seq,)),
                        dma((n_tp,)), dma((n_tp - 1,)), dma((n_tp - 1,))],
        compiler_params=pltpu.CompilerParams(collective_id=0, has_side_effects=True,
                                             vmem_limit_bytes=58 << 20),
        cost_estimate=pl.CostEstimate(flops=10 ** 10, bytes_accessed=3 * 10 ** 7,
                                      transcendentals=10 ** 6),
    )(page_table, cache_len, tree_mask.reshape(n_seq, rows, n_draft), draft_q, draft_kv, kv_pool,
      out_weight)

    accepted_kv, layer_out = pl.pallas_call(
        accept_kernel,
        out_shape=(jax.ShapeDtypeStruct((2, n_req, page_len, width), bf16),
                   jax.ShapeDtypeStruct((rows, out_w), bf16)),
        in_specs=[VMEM, ANY, ANY],
        out_specs=(ANY, ANY),
        scratch_shapes=[pltpu.VMEM((n_req, 2, n_draft, width), bf16),
                        pltpu.VMEM((n_req, 2, n_draft, width), bf16),
                        pltpu.VMEM((page_len - n_draft, width), bf16),
                        dma((n_req, 2, group)), dma((n_req, 2)), dma((n_req, 2)), dma((1,))],
        compiler_params=pltpu.CompilerParams(vmem_limit_bytes=58 << 20),
    )(accepted_rows, kv_all.reshape(n_req, group, 2, rows, width), layer)
    return (layer_out, accepted_kv)


def solution(mesh):
    return jax.shard_map(
        body,
        mesh=mesh,
        in_specs=(P("seq", "tp"), P(None, "seq", "tp"), P(None, "seq", None, "tp"),
                  P(), P(), P(), P(), P("tp", None)),
        out_specs=(P("seq", "tp"), P(None, None, None, "tp")),
        check_vma=False,
    )
```

```python
import functools
import math

import jax
import jax.numpy as jnp
from jax import lax
from jax.experimental import pallas as pl
from jax.experimental.pallas import tpu as pltpu
from jax.sharding import PartitionSpec as P

HD = 128
NEGATIVE = -1e30
MESH = pl.DeviceIdType.MESH
ANY = pl.BlockSpec(memory_space=pl.ANY)
VMEM = pl.BlockSpec(memory_space=pltpu.VMEM)
SMEM = pl.BlockSpec(memory_space=pltpu.SMEM)
NT = (((1,), (1,)), ((), ()))


def fused_kernel(n_req, n_pages, n_seq, n_tp, group, table, cache_len, mask, q, kv, pool, weight,
                 out, kva,
                 qa, kbuf, vbuf, m_st, l_st, acc_st, part, stat, got, gstat, kg, wbuf, att, tree,
                 pbuf, prbuf, last, code,
                 qsem, qrsem, fsem, cssem, crsem, cfsem, lsem, ksem, vsem, gsem,
                 asem, arsem, tsem, trsem, wsem, psem, prsem):
    me = lax.axis_index("seq")
    tp = lax.axis_index("tp")
    grp = me // group
    inner = lax.rem(me, group)
    n_slots, page_len, width = kbuf.shape
    rows = qa.shape[1] // group
    n_draft = qa.shape[1]
    heads = width // HD
    out_w = out.shape[1]
    scale = 1.0 / math.sqrt(HD)

    def across(d):
        return lax.rem(grp + d, n_req) * group + inner

    def other(d):
        return grp * group + lax.rem(inner + d, group)

    def remote(a, b, s, r, where):
        return pltpu.make_async_remote_copy(
            src_ref=a, dst_ref=b, send_sem=s, recv_sem=r, device_id=where, device_id_type=MESH)

    def block(i):
        return qa.at[i // group, pl.ds(pl.multiple_of(lax.rem(i, group) * rows, rows), rows)]

    barrier = pltpu.get_barrier_semaphore()
    for d in range(1, n_seq):
        pl.semaphore_signal(barrier, inc=1, device_id={"seq": lax.rem(me + d, n_seq)},
                            device_id_type=MESH)
    for d in range(1, n_tp):
        pl.semaphore_signal(barrier, inc=1, device_id={"tp": lax.rem(tp + d, n_tp)},
                            device_id_type=MESH)
    own_q = pltpu.make_async_copy(q, block(me), lsem.at[0])
    own_q.start()
    own_kv = pltpu.make_async_copy(kv, kva.at[me], lsem.at[1])
    own_kv.start()
    m_st[0] = jnp.full(m_st.shape[1:], NEGATIVE, jnp.float32)
    l_st[0] = jnp.zeros(l_st.shape[1:], jnp.float32)
    acc_st[0] = jnp.zeros(acc_st.shape[1:], jnp.float32)
    for r in range(n_req):
        last[r] = 0
    pl.semaphore_wait(barrier, n_seq + n_tp - 2)

    sent = []

    def send(*args):
        c = remote(*args)
        c.start()
        sent.append(c)

    for d in range(n_req - 1, 0, -1):
        send(q, block(me), qsem.at[d - 1], qrsem.at[me], {"seq": across(d)})
    for d in range(1, group):
        send(q, block(me), qsem.at[n_req - 2 + d], qrsem.at[me], {"seq": other(d)})
    def q_arrived(b):
        remote(q, block(b), qsem.at[0], qrsem.at[b], {"seq": other(1)}).wait_recv()

    def kv_arrived(b):
        remote(kv, kva.at[b], cssem.at[0], crsem.at[b], {"seq": other(1)}).wait_recv()

    for s in range(n_slots):
        pltpu.make_async_copy(pool.at[0, s], kbuf.at[s], ksem.at[s]).start()
        pltpu.make_async_copy(pool.at[1, s], vbuf.at[s], vsem.at[s]).start()
    loads = []
    for t in range(n_tp):
        c = pltpu.make_async_copy(weight.at[:, pl.ds(t * out_w, out_w)], wbuf.at[t], wsem.at[t])
        c.start()
        loads.append(c)
    shape = table.shape
    number = (lax.broadcasted_iota(jnp.int32, shape, 0) * n_pages
              + lax.broadcasted_iota(jnp.int32, shape, 1) + 1)
    for s in range(n_slots):
        code[s] = jnp.sum(jnp.where(table[...] == me * n_slots + s, number, 0))

    for e in range(1, n_req):
        b = across(e)
        q_arrived(b)
        for d in range(1, group):
            send(block(b), block(b), fsem.at[(e - 1) * (group - 1) + d - 1], qrsem.at[b],
                 {"seq": other(d)})
    for d in range(1, group):
        send(kv, kva.at[me], cssem.at[n_req - 2 + d], crsem.at[me], {"seq": other(d)})
    for d in range(n_req - 1, 0, -1):
        send(kv, kva.at[me], cssem.at[d - 1], crsem.at[me], {"seq": across(d)})
    for d in range(1, group):
        q_arrived(other(d))
        for e in range(1, n_req):
            q_arrived(lax.rem(grp + e, n_req) * group + lax.rem(inner + d, group))
    own_q.wait()

    def forward(e, d, start):
        b = across(e)
        c = remote(kva.at[b], kva.at[b], cfsem.at[(e - 1) * (group - 1) + d - 1], crsem.at[b],
                   {"seq": other(d)})
        if start:
            c.start()
        else:
            c.wait_send()

    def step(s, carry):
        pltpu.make_async_copy(pool.at[0, s], kbuf.at[s], ksem.at[s]).wait()
        pltpu.make_async_copy(pool.at[1, s], vbuf.at[s], vsem.at[s]).wait()
        number = code[s]
        place = jnp.maximum(number - 1, 0)
        r = jnp.minimum(lax.div(place, n_pages), n_req - 1)
        left = jnp.where(number > 0, cache_len[r] - (place - r * n_pages) * page_len, 0)
        prev = last[r]
        scores = []
        for h in range(heads):
            cols = slice(h * HD, (h + 1) * HD)
            scores.append(lax.dot_general(
                qa[r, :, cols], kbuf[s, :, cols], NT, preferred_element_type=jnp.float32))
        live = lax.broadcasted_iota(jnp.int32, scores[0].shape, 1) < left
        probs = []
        scales = []
        for h in range(heads):
            x = jnp.where(live, scores[h] * scale, NEGATIVE)
            old = m_st[prev, h]
            new = jnp.maximum(old, jnp.max(x, axis=1, keepdims=True))
            p = jnp.exp(x - new)
            a = jnp.exp(old - new)
            m_st[s + 1, h] = new
            l_st[s + 1, h] = a * l_st[prev, h] + jnp.sum(p, axis=1, keepdims=True)
            probs.append(p.astype(jnp.bfloat16))
            scales.append(a)
        for h in range(heads):
            cols = slice(h * HD, (h + 1) * HD)
            o = jnp.dot(probs[h], vbuf[s, :, cols], preferred_element_type=jnp.float32)
            acc_st[s + 1, :, cols] = scales[h] * acc_st[prev, :, cols] + o
        for i in range(n_req):
            last[i] = jnp.where((left > 0) & (r == i), s + 1, last[i])
        return carry

    lax.fori_loop(0, n_slots, step, 0)

    lane = lax.broadcasted_iota(jnp.int32, (n_draft, HD), 1)
    for r in range(n_req):
        at = last[r]
        acc = acc_st[at].astype(jnp.bfloat16)
        info = jnp.zeros((n_draft, HD), jnp.float32)
        for h in range(heads):
            info = jnp.where(lane == h, m_st[at, h], info)
            info = jnp.where(lane == HD // 2 + h, l_st[at, h], info)
        for g in range(group):
            part[r * group + g] = acc[g * rows:(g + 1) * rows]
            stat[r * group + g] = info[g * rows:(g + 1) * rows]
    own_part = pltpu.make_async_copy(part.at[me], got.at[me], lsem.at[2])
    own_stat = pltpu.make_async_copy(stat.at[me], gstat.at[me], lsem.at[3])
    own_part.start()
    own_stat.start()
    for d in range(1, n_seq):
        peer = lax.rem(me + d, n_seq)
        send(stat.at[peer], gstat.at[me], tsem.at[d - 1], trsem.at[me], {"seq": peer})
        send(part.at[peer], got.at[me], asem.at[d - 1], arsem.at[me], {"seq": peer})

    for e in range(1, n_req):
        kv_arrived(across(e))
        for d in range(1, group):
            forward(e, d, True)

    own_kv.wait()
    for d in range(1, group):
        kv_arrived(other(d))
    tree_in = []
    for g in range(group):
        c = pltpu.make_async_copy(kva.at[grp * group + g], kg.at[g], gsem.at[g])
        c.start()
        tree_in.append(c)
    for c in tree_in:
        c.wait()
    allowed = mask[me] == 1
    mine = qa[grp, pl.ds(pl.multiple_of(inner * rows, rows), rows), :]
    tree_m = []
    tree_l = []
    for h in range(heads):
        cols = slice(h * HD, (h + 1) * HD)
        keys = jnp.concatenate([kg[g, 0, :, cols] for g in range(group)], axis=0)
        values = jnp.concatenate([kg[g, 1, :, cols] for g in range(group)], axis=0)
        x = lax.dot_general(mine[:, cols], keys, NT, preferred_element_type=jnp.float32) * scale
        x = jnp.where(allowed, x, NEGATIVE)
        top = jnp.max(x, axis=1, keepdims=True)
        p = jnp.where(allowed, jnp.exp(x - top), 0.0)
        tree_m.append(top)
        tree_l.append(jnp.sum(p, axis=1, keepdims=True))
        tree[:, cols] = jnp.dot(p.astype(jnp.bfloat16), values, preferred_element_type=jnp.float32)

    own_part.wait()
    own_stat.wait()
    for d in range(1, n_seq):
        i = lax.rem(me + n_seq - d, n_seq)
        remote(stat.at[i], gstat.at[i], tsem.at[d - 1], trsem.at[i], {"seq": i}).wait_recv()
        remote(part.at[i], got.at[i], asem.at[d - 1], arsem.at[i], {"seq": i}).wait_recv()
    for h in range(heads):
        cols = slice(h * HD, (h + 1) * HD)
        top = tree_m[h]
        for i in range(n_seq):
            top = jnp.maximum(top, gstat[i, :, h:h + 1])
        f = jnp.exp(tree_m[h] - top)
        den = f * tree_l[h]
        num = f * tree[:, cols]
        for i in range(n_seq):
            f = jnp.exp(gstat[i, :, h:h + 1] - top)
            den = den + f * gstat[i, :, HD // 2 + h:HD // 2 + h + 1]
            num = num + f * got[i, :, cols].astype(jnp.float32)
        att[:, cols] = (num / den).astype(jnp.bfloat16)
    for c in loads:
        c.wait()
    for d in range(1, n_tp):
        peer = lax.rem(tp + d, n_tp)
        pbuf[d - 1] = jnp.dot(att[...], wbuf[peer],
                              preferred_element_type=jnp.float32).astype(jnp.bfloat16)
        c = pltpu.make_async_remote_copy(
            src_ref=pbuf.at[d - 1], dst_ref=prbuf.at[d - 1], send_sem=psem.at[d - 1],
            recv_sem=prsem.at[d - 1], device_id={"tp": peer}, device_id_type=MESH)
        c.start()
        sent.append(c)
    total = jnp.dot(att[...], wbuf[tp], preferred_element_type=jnp.float32)
    for d in range(1, n_tp):
        pltpu.make_async_remote_copy(
            src_ref=pbuf.at[d - 1], dst_ref=prbuf.at[d - 1], send_sem=psem.at[d - 1],
            recv_sem=prsem.at[d - 1], device_id={"tp": lax.rem(tp + d, n_tp)},
            device_id_type=MESH).wait_recv()
        total = total + prbuf[d - 1].astype(jnp.float32)
    out[...] = total.astype(out.dtype)
    for d in range(1, group):
        for e in range(1, n_req):
            kv_arrived(lax.rem(grp + e, n_req) * group + lax.rem(inner + d, group))
    for e in range(1, n_req):
        for d in range(1, group):
            forward(e, d, False)
    for c in sent:
        c.wait_send()


def accept_kernel(rows_ref, kv, layer, out, layer_out, blocks, picked, zeros, isem, osem, zsem, lsem):
    n_req, group, _, rows, width = kv.shape
    n_draft = group * rows
    copies = []

    def copy(a, b, sem):
        c = pltpu.make_async_copy(a, b, sem)
        c.start()
        return c

    loads = []
    for r in range(n_req):
        for c in range(2):
            loads.append([copy(kv.at[r, g, c], blocks.at[r, c, pl.ds(g * rows, rows)],
                               isem.at[r, c, g]) for g in range(group)])
    copies.append(copy(layer, layer_out, lsem.at[0]))
    zeros[...] = jnp.zeros(zeros.shape, zeros.dtype)
    for r in range(n_req):
        for c in range(2):
            copies.append(copy(zeros, out.at[c, r, pl.ds(n_draft, zeros.shape[0])], zsem.at[r, c]))
    for r in range(n_req):
        pick = (lax.broadcasted_iota(jnp.int32, (n_draft, n_draft), 0)
                == rows_ref[r:r + 1, :]).astype(jnp.bfloat16)
        for c in range(2):
            for load in loads[2 * r + c]:
                load.wait()
            picked[r, c] = lax.dot_general(
                pick, blocks[r, c], (((0,), (0,)), ((), ())),
                preferred_element_type=jnp.float32).astype(out.dtype)
            copies.append(copy(picked.at[r, c], out.at[c, r, pl.ds(0, n_draft)], osem.at[r, c]))
    for c in copies:
        c.wait()


def body(draft_q, draft_kv, kv_pool, page_table, cache_len, tree_mask, accepted_rows, out_weight):
    n_seq = lax.axis_size("seq")
    n_tp = lax.axis_size("tp")
    rows, width = draft_q.shape
    heads = width // HD
    n_req, n_pages = page_table.shape
    n_draft = tree_mask.shape[1]
    n_slots, page_len = kv_pool.shape[1:3]
    group = n_seq // n_req
    out_w = out_weight.shape[1] // n_tp
    bf16, f32 = jnp.bfloat16, jnp.float32
    dma = pltpu.SemaphoreType.DMA

    layer, kv_all = pl.pallas_call(
        functools.partial(fused_kernel, n_req, n_pages, n_seq, n_tp, group),
        out_shape=(jax.ShapeDtypeStruct((rows, out_w), bf16),
                   jax.ShapeDtypeStruct((n_seq, 2, rows, width), bf16)),
        in_specs=[VMEM, SMEM, VMEM, ANY, ANY, ANY, ANY],
        out_specs=(VMEM, ANY),
        scratch_shapes=[pltpu.VMEM((n_req, n_draft, width), bf16),
                        pltpu.VMEM((n_slots, page_len, width), bf16),
                        pltpu.VMEM((n_slots, page_len, width), bf16),
                        pltpu.VMEM((n_slots + 1, heads, n_draft, HD), f32),
                        pltpu.VMEM((n_slots + 1, heads, n_draft, HD), f32),
                        pltpu.VMEM((n_slots + 1, n_draft, width), f32),
                        pltpu.VMEM((n_seq, rows, width), bf16),
                        pltpu.VMEM((n_seq, rows, HD), f32),
                        pltpu.VMEM((n_seq, rows, width), bf16),
                        pltpu.VMEM((n_seq, rows, HD), f32),
                        pltpu.VMEM((group, 2, rows, width), bf16),
                        pltpu.VMEM((n_tp, width, out_w), bf16),
                        pltpu.VMEM((rows, width), bf16),
                        pltpu.VMEM((rows, width), f32),
                        pltpu.VMEM((n_tp - 1, rows, out_w), bf16),
                        pltpu.VMEM((n_tp - 1, rows, out_w), bf16),
                        pltpu.SMEM((n_req,), jnp.int32), pltpu.SMEM((n_slots,), jnp.int32),
                        dma((n_req + group - 2,)), dma((n_seq,)),
                        dma(((n_req - 1) * (group - 1),)),
                        dma((n_req + group - 2,)), dma((n_seq,)),
                        dma(((n_req - 1) * (group - 1),)),
                        dma((4,)), dma((n_slots,)), dma((n_slots,)), dma((group,)),
                        dma((n_seq - 1,)), dma((n_seq,)), dma((n_seq - 1,)), dma((n_seq,)),
                        dma((n_tp,)), dma((n_tp - 1,)), dma((n_tp - 1,))],
        compiler_params=pltpu.CompilerParams(collective_id=0, has_side_effects=True,
                                             vmem_limit_bytes=58 << 20),
        cost_estimate=pl.CostEstimate(flops=10 ** 10, bytes_accessed=3 * 10 ** 7,
                                      transcendentals=10 ** 6),
    )(page_table, cache_len, tree_mask.reshape(n_seq, rows, n_draft), draft_q, draft_kv, kv_pool,
      out_weight)

    accepted_kv, layer_out = pl.pallas_call(
        accept_kernel,
        out_shape=(jax.ShapeDtypeStruct((2, n_req, page_len, width), bf16),
                   jax.ShapeDtypeStruct((rows, out_w), bf16)),
        in_specs=[VMEM, ANY, ANY],
        out_specs=(ANY, ANY),
        scratch_shapes=[pltpu.VMEM((n_req, 2, n_draft, width), bf16),
                        pltpu.VMEM((n_req, 2, n_draft, width), bf16),
                        pltpu.VMEM((page_len - n_draft, width), bf16),
                        dma((n_req, 2, group)), dma((n_req, 2)), dma((n_req, 2)), dma((1,))],
        compiler_params=pltpu.CompilerParams(vmem_limit_bytes=58 << 20),
    )(accepted_rows, kv_all.reshape(n_req, group, 2, rows, width), layer)
    return (layer_out, accepted_kv)


def solution(mesh):
    return jax.shard_map(
        body,
        mesh=mesh,
        in_specs=(P("seq", "tp"), P(None, "seq", "tp"), P(None, "seq", None, "tp"),
                  P(), P(), P(), P(), P("tp", None)),
        out_specs=(P("seq", "tp"), P(None, None, None, "tp")),
        check_vma=False,
    )
```

```python
import functools
import math

import jax
import jax.numpy as jnp
from jax import lax
from jax.experimental import pallas as pl
from jax.experimental.pallas import tpu as pltpu
from jax.sharding import PartitionSpec as P

HD = 128
NEGATIVE = -1e30
MESH = pl.DeviceIdType.MESH
ANY = pl.BlockSpec(memory_space=pl.ANY)
VMEM = pl.BlockSpec(memory_space=pltpu.VMEM)
SMEM = pl.BlockSpec(memory_space=pltpu.SMEM)
NT = (((1,), (1,)), ((), ()))


def fused_kernel(n_req, n_pages, n_seq, n_tp, group, table, cache_len, mask, accepted, q, kv, pool, weight,
                 out, acc_kv,
                 kva, picked, zeros, qa, kbuf, vbuf, m_st, l_st, acc_st, part, stat, got, gstat, wbuf, att, tree,
                 pbuf, prbuf, last, code,
                 qsem, qrsem, fsem, cssem, crsem, cfsem, lsem, ksem, vsem, osem, zsem,
                 asem, arsem, tsem, trsem, wsem, psem, prsem):
    me = lax.axis_index("seq")
    tp = lax.axis_index("tp")
    grp = me // group
    inner = lax.rem(me, group)
    n_slots, page_len, width = kbuf.shape
    rows = qa.shape[1] // group
    n_draft = qa.shape[1]
    heads = width // HD
    out_w = out.shape[1]
    scale = 1.0 / math.sqrt(HD)

    def across(d):
        return lax.rem(grp + d, n_req) * group + inner

    def other(d):
        return grp * group + lax.rem(inner + d, group)

    def remote(a, b, s, r, where):
        return pltpu.make_async_remote_copy(
            src_ref=a, dst_ref=b, send_sem=s, recv_sem=r, device_id=where, device_id_type=MESH)

    def block(i):
        return qa.at[i // group, pl.ds(pl.multiple_of(lax.rem(i, group) * rows, rows), rows)]

    barrier = pltpu.get_barrier_semaphore()
    for d in range(1, n_seq):
        pl.semaphore_signal(barrier, inc=1, device_id={"seq": lax.rem(me + d, n_seq)},
                            device_id_type=MESH)
    for d in range(1, n_tp):
        pl.semaphore_signal(barrier, inc=1, device_id={"tp": lax.rem(tp + d, n_tp)},
                            device_id_type=MESH)
    own_q = pltpu.make_async_copy(q, block(me), lsem.at[0])
    own_q.start()
    own_kv = pltpu.make_async_copy(kv, kva.at[me], lsem.at[1])
    own_kv.start()
    m_st[0] = jnp.full(m_st.shape[1:], NEGATIVE, jnp.float32)
    l_st[0] = jnp.zeros(l_st.shape[1:], jnp.float32)
    acc_st[0] = jnp.zeros(acc_st.shape[1:], jnp.float32)
    for r in range(n_req):
        last[r] = 0
    pl.semaphore_wait(barrier, n_seq + n_tp - 2)

    sent = []

    def send(*args):
        c = remote(*args)
        c.start()
        sent.append(c)

    for d in range(n_req - 1, 0, -1):
        send(q, block(me), qsem.at[d - 1], qrsem.at[me], {"seq": across(d)})
    for d in range(1, group):
        send(q, block(me), qsem.at[n_req - 2 + d], qrsem.at[me], {"seq": other(d)})
    def q_arrived(b):
        remote(q, block(b), qsem.at[0], qrsem.at[b], {"seq": other(1)}).wait_recv()

    def kv_arrived(b):
        remote(kv, kva.at[b], cssem.at[0], crsem.at[b], {"seq": other(1)}).wait_recv()

    for s in range(n_slots):
        pltpu.make_async_copy(pool.at[0, s], kbuf.at[s], ksem.at[s]).start()
        pltpu.make_async_copy(pool.at[1, s], vbuf.at[s], vsem.at[s]).start()
    loads = []
    for t in range(n_tp):
        c = pltpu.make_async_copy(weight.at[:, pl.ds(t * out_w, out_w)], wbuf.at[t], wsem.at[t])
        c.start()
        loads.append(c)
    zeros[...] = jnp.zeros(zeros.shape, zeros.dtype)
    writes = []
    for r in range(n_req):
        for c in range(2):
            writes.append(pltpu.make_async_copy(
                zeros, acc_kv.at[c, r, pl.ds(n_draft, zeros.shape[0])], zsem.at[r, c]))
            writes[-1].start()
    shape = table.shape
    number = (lax.broadcasted_iota(jnp.int32, shape, 0) * n_pages
              + lax.broadcasted_iota(jnp.int32, shape, 1) + 1)
    for s in range(n_slots):
        code[s] = jnp.sum(jnp.where(table[...] == me * n_slots + s, number, 0))

    for e in range(1, n_req):
        b = across(e)
        q_arrived(b)
        for d in range(1, group):
            send(block(b), block(b), fsem.at[(e - 1) * (group - 1) + d - 1], qrsem.at[b],
                 {"seq": other(d)})
    for d in range(1, group):
        send(kv, kva.at[me], cssem.at[n_req - 2 + d], crsem.at[me], {"seq": other(d)})
    for d in range(n_req - 1, 0, -1):
        send(kv, kva.at[me], cssem.at[d - 1], crsem.at[me], {"seq": across(d)})
    for d in range(1, group):
        q_arrived(other(d))
        for e in range(1, n_req):
            q_arrived(lax.rem(grp + e, n_req) * group + lax.rem(inner + d, group))
    own_q.wait()

    def forward(e, d, start):
        b = across(e)
        c = remote(kva.at[b], kva.at[b], cfsem.at[(e - 1) * (group - 1) + d - 1], crsem.at[b],
                   {"seq": other(d)})
        if start:
            c.start()
        else:
            c.wait_send()

    def step(s, carry):
        pltpu.make_async_copy(pool.at[0, s], kbuf.at[s], ksem.at[s]).wait()
        pltpu.make_async_copy(pool.at[1, s], vbuf.at[s], vsem.at[s]).wait()
        number = code[s]
        place = jnp.maximum(number - 1, 0)
        r = jnp.minimum(lax.div(place, n_pages), n_req - 1)
        left = jnp.where(number > 0, cache_len[r] - (place - r * n_pages) * page_len, 0)
        prev = last[r]
        scores = []
        for h in range(heads):
            cols = slice(h * HD, (h + 1) * HD)
            scores.append(lax.dot_general(
                qa[r, :, cols], kbuf[s, :, cols], NT, preferred_element_type=jnp.float32))
        live = lax.broadcasted_iota(jnp.int32, scores[0].shape, 1) < left
        probs = []
        scales = []
        for h in range(heads):
            x = jnp.where(live, scores[h] * scale, NEGATIVE)
            old = m_st[prev, h]
            new = jnp.maximum(old, jnp.max(x, axis=1, keepdims=True))
            p = jnp.exp(x - new)
            a = jnp.exp(old - new)
            m_st[s + 1, h] = new
            l_st[s + 1, h] = a * l_st[prev, h] + jnp.sum(p, axis=1, keepdims=True)
            probs.append(p.astype(jnp.bfloat16))
            scales.append(a)
        for h in range(heads):
            cols = slice(h * HD, (h + 1) * HD)
            o = jnp.dot(probs[h], vbuf[s, :, cols], preferred_element_type=jnp.float32)
            acc_st[s + 1, :, cols] = scales[h] * acc_st[prev, :, cols] + o
        for i in range(n_req):
            last[i] = jnp.where((left > 0) & (r == i), s + 1, last[i])
        return carry

    lax.fori_loop(0, n_slots, step, 0)

    lane = lax.broadcasted_iota(jnp.int32, (n_draft, HD), 1)
    for r in range(n_req):
        at = last[r]
        acc = acc_st[at].astype(jnp.bfloat16)
        info = jnp.zeros((n_draft, HD), jnp.float32)
        for h in range(heads):
            info = jnp.where(lane == h, m_st[at, h], info)
            info = jnp.where(lane == HD // 2 + h, l_st[at, h], info)
        for g in range(group):
            part[r * group + g] = acc[g * rows:(g + 1) * rows]
            stat[r * group + g] = info[g * rows:(g + 1) * rows]
    own_part = pltpu.make_async_copy(part.at[me], got.at[me], lsem.at[2])
    own_stat = pltpu.make_async_copy(stat.at[me], gstat.at[me], lsem.at[3])
    own_part.start()
    own_stat.start()
    for d in range(1, n_seq):
        peer = lax.rem(me + d, n_seq)
        send(stat.at[peer], gstat.at[me], tsem.at[d - 1], trsem.at[me], {"seq": peer})
        send(part.at[peer], got.at[me], asem.at[d - 1], arsem.at[me], {"seq": peer})

    for e in range(1, n_req):
        kv_arrived(across(e))
        for d in range(1, group):
            forward(e, d, True)

    own_kv.wait()
    for d in range(1, group):
        kv_arrived(other(d))
    allowed = mask[me] == 1
    mine = qa[grp, pl.ds(pl.multiple_of(inner * rows, rows), rows), :]
    tree_m = []
    tree_l = []
    for h in range(heads):
        cols = slice(h * HD, (h + 1) * HD)
        keys = jnp.concatenate([kva[grp * group + g, 0, :, cols] for g in range(group)], axis=0)
        values = jnp.concatenate([kva[grp * group + g, 1, :, cols] for g in range(group)], axis=0)
        x = lax.dot_general(mine[:, cols], keys, NT, preferred_element_type=jnp.float32) * scale
        x = jnp.where(allowed, x, NEGATIVE)
        top = jnp.max(x, axis=1, keepdims=True)
        p = jnp.where(allowed, jnp.exp(x - top), 0.0)
        tree_m.append(top)
        tree_l.append(jnp.sum(p, axis=1, keepdims=True))
        tree[:, cols] = jnp.dot(p.astype(jnp.bfloat16), values, preferred_element_type=jnp.float32)

    own_part.wait()
    own_stat.wait()
    for d in range(1, n_seq):
        i = lax.rem(me + n_seq - d, n_seq)
        remote(stat.at[i], gstat.at[i], tsem.at[d - 1], trsem.at[i], {"seq": i}).wait_recv()
        remote(part.at[i], got.at[i], asem.at[d - 1], arsem.at[i], {"seq": i}).wait_recv()
    for h in range(heads):
        cols = slice(h * HD, (h + 1) * HD)
        top = tree_m[h]
        for i in range(n_seq):
            top = jnp.maximum(top, gstat[i, :, h:h + 1])
        f = jnp.exp(tree_m[h] - top)
        den = f * tree_l[h]
        num = f * tree[:, cols]
        for i in range(n_seq):
            f = jnp.exp(gstat[i, :, h:h + 1] - top)
            den = den + f * gstat[i, :, HD // 2 + h:HD // 2 + h + 1]
            num = num + f * got[i, :, cols].astype(jnp.float32)
        att[:, cols] = (num / den).astype(jnp.bfloat16)
    for c in loads:
        c.wait()
    for d in range(1, n_tp):
        peer = lax.rem(tp + d, n_tp)
        pbuf[d - 1] = jnp.dot(att[...], wbuf[peer],
                              preferred_element_type=jnp.float32).astype(jnp.bfloat16)
        c = pltpu.make_async_remote_copy(
            src_ref=pbuf.at[d - 1], dst_ref=prbuf.at[d - 1], send_sem=psem.at[d - 1],
            recv_sem=prsem.at[d - 1], device_id={"tp": peer}, device_id_type=MESH)
        c.start()
        sent.append(c)
    total = jnp.dot(att[...], wbuf[tp], preferred_element_type=jnp.float32)
    for d in range(1, group):
        for e in range(1, n_req):
            kv_arrived(lax.rem(grp + e, n_req) * group + lax.rem(inner + d, group))
    for r in range(n_req):
        pick = (lax.broadcasted_iota(jnp.int32, (n_draft, n_draft), 0)
                == accepted[r:r + 1, :]).astype(jnp.bfloat16)
        for c in range(2):
            blocks = jnp.concatenate([kva[r * group + g, c] for g in range(group)], axis=0)
            picked[r, c] = lax.dot_general(
                pick, blocks, (((0,), (0,)), ((), ())),
                preferred_element_type=jnp.float32).astype(jnp.bfloat16)
            writes.append(pltpu.make_async_copy(
                picked.at[r, c], acc_kv.at[c, r, pl.ds(0, n_draft)], osem.at[r, c]))
            writes[-1].start()
    for d in range(1, n_tp):
        pltpu.make_async_remote_copy(
            src_ref=pbuf.at[d - 1], dst_ref=prbuf.at[d - 1], send_sem=psem.at[d - 1],
            recv_sem=prsem.at[d - 1], device_id={"tp": lax.rem(tp + d, n_tp)},
            device_id_type=MESH).wait_recv()
        total = total + prbuf[d - 1].astype(jnp.float32)
    out[...] = total.astype(out.dtype)
    for e in range(1, n_req):
        for d in range(1, group):
            forward(e, d, False)
    for c in writes:
        c.wait()
    for c in sent:
        c.wait_send()


def copy_kernel(accepted, layer, out, layer_out, sem):
    halves, n_req = accepted.shape[:2]
    copies = [pltpu.make_async_copy(layer, layer_out, sem.at[halves * n_req])]
    for c in range(halves):
        for r in range(n_req):
            copies.append(pltpu.make_async_copy(
                accepted.at[c, r], out.at[c, r], sem.at[c * n_req + r]))
    for c in copies:
        c.start()
    for c in copies:
        c.wait()


def body(draft_q, draft_kv, kv_pool, page_table, cache_len, tree_mask, accepted_rows, out_weight):
    n_seq = lax.axis_size("seq")
    n_tp = lax.axis_size("tp")
    rows, width = draft_q.shape
    heads = width // HD
    n_req, n_pages = page_table.shape
    n_draft = tree_mask.shape[1]
    n_slots, page_len = kv_pool.shape[1:3]
    group = n_seq // n_req
    out_w = out_weight.shape[1] // n_tp
    bf16, f32 = jnp.bfloat16, jnp.float32
    dma = pltpu.SemaphoreType.DMA

    layer, accepted_block = pl.pallas_call(
        functools.partial(fused_kernel, n_req, n_pages, n_seq, n_tp, group),
        out_shape=(jax.ShapeDtypeStruct((rows, out_w), bf16),
                   jax.ShapeDtypeStruct((2, n_req, page_len, width), bf16)),
        in_specs=[VMEM, SMEM, VMEM, VMEM, ANY, ANY, ANY, ANY],
        out_specs=(VMEM, ANY),
        scratch_shapes=[pltpu.VMEM((n_seq, 2, rows, width), bf16),
                        pltpu.VMEM((n_req, 2, n_draft, width), bf16),
                        pltpu.VMEM((page_len - n_draft, width), bf16),
                        pltpu.VMEM((n_req, n_draft, width), bf16),
                        pltpu.VMEM((n_slots, page_len, width), bf16),
                        pltpu.VMEM((n_slots, page_len, width), bf16),
                        pltpu.VMEM((n_slots + 1, heads, n_draft, HD), f32),
                        pltpu.VMEM((n_slots + 1, heads, n_draft, HD), f32),
                        pltpu.VMEM((n_slots + 1, n_draft, width), f32),
                        pltpu.VMEM((n_seq, rows, width), bf16),
                        pltpu.VMEM((n_seq, rows, HD), f32),
                        pltpu.VMEM((n_seq, rows, width), bf16),
                        pltpu.VMEM((n_seq, rows, HD), f32),
                        pltpu.VMEM((n_tp, width, out_w), bf16),
                        pltpu.VMEM((rows, width), bf16),
                        pltpu.VMEM((rows, width), f32),
                        pltpu.VMEM((n_tp - 1, rows, out_w), bf16),
                        pltpu.VMEM((n_tp - 1, rows, out_w), bf16),
                        pltpu.SMEM((n_req,), jnp.int32), pltpu.SMEM((n_slots,), jnp.int32),
                        dma((n_req + group - 2,)), dma((n_seq,)),
                        dma(((n_req - 1) * (group - 1),)),
                        dma((n_req + group - 2,)), dma((n_seq,)),
                        dma(((n_req - 1) * (group - 1),)),
                        dma((4,)), dma((n_slots,)), dma((n_slots,)), dma((n_req, 2)), dma((n_req, 2)),
                        dma((n_seq - 1,)), dma((n_seq,)), dma((n_seq - 1,)), dma((n_seq,)),
                        dma((n_tp,)), dma((n_tp - 1,)), dma((n_tp - 1,))],
        compiler_params=pltpu.CompilerParams(collective_id=0, has_side_effects=True,
                                             vmem_limit_bytes=58 << 20),
        cost_estimate=pl.CostEstimate(flops=10 ** 10, bytes_accessed=3 * 10 ** 7,
                                      transcendentals=10 ** 6),
    )(page_table, cache_len, tree_mask.reshape(n_seq, rows, n_draft), accepted_rows, draft_q, draft_kv, kv_pool,
      out_weight)

    accepted_kv, layer_out = pl.pallas_call(
        copy_kernel,
        out_shape=(jax.ShapeDtypeStruct((2, n_req, page_len, width), bf16),
                   jax.ShapeDtypeStruct((rows, out_w), bf16)),
        in_specs=[ANY, ANY],
        out_specs=(ANY, ANY),
        scratch_shapes=[dma((2 * n_req + 1,))],
        compiler_params=pltpu.CompilerParams(vmem_limit_bytes=58 << 20),
    )(accepted_block, layer)
    return (layer_out, accepted_kv)


def solution(mesh):
    return jax.shard_map(
        body,
        mesh=mesh,
        in_specs=(P("seq", "tp"), P(None, "seq", "tp"), P(None, "seq", None, "tp"),
                  P(), P(), P(), P(), P("tp", None)),
        out_specs=(P("seq", "tp"), P(None, None, None, "tp")),
        check_vma=False,
    )
```

```python
import functools
import math

import jax
import jax.numpy as jnp
from jax import lax
from jax.experimental import pallas as pl
from jax.experimental.pallas import tpu as pltpu
from jax.sharding import PartitionSpec as P

HD = 128
NEGATIVE = -1e30
MESH = pl.DeviceIdType.MESH
ANY = pl.BlockSpec(memory_space=pl.ANY)
VMEM = pl.BlockSpec(memory_space=pltpu.VMEM)
SMEM = pl.BlockSpec(memory_space=pltpu.SMEM)
NT = (((1,), (1,)), ((), ()))


def fused_kernel(n_req, n_pages, n_seq, n_tp, group, table, cache_len, mask, accepted, q, kv, pool, weight,
                 out, acc_kv,
                 kva, picked, zeros, qa, kbuf, vbuf, m_st, l_st, acc_st, part, stat, got, gstat, wbuf, att, tree,
                 pbuf, prbuf, last, code,
                 qsem, qrsem, fsem, cssem, crsem, cfsem, lsem, ksem, vsem, osem, zsem,
                 asem, arsem, tsem, trsem, wsem, psem, prsem):
    me = lax.axis_index("seq")
    tp = lax.axis_index("tp")
    grp = me // group
    inner = lax.rem(me, group)
    n_slots, page_len, width = kbuf.shape
    rows = qa.shape[1] // group
    n_draft = qa.shape[1]
    heads = width // HD
    out_w = out.shape[1]
    scale = 1.0 / math.sqrt(HD)

    def across(d):
        return lax.rem(grp + d, n_req) * group + inner

    def other(d):
        return grp * group + lax.rem(inner + d, group)

    def remote(a, b, s, r, where):
        return pltpu.make_async_remote_copy(
            src_ref=a, dst_ref=b, send_sem=s, recv_sem=r, device_id=where, device_id_type=MESH)

    def block(i):
        return qa.at[i // group, pl.ds(pl.multiple_of(lax.rem(i, group) * rows, rows), rows)]

    barrier = pltpu.get_barrier_semaphore()
    for d in range(1, n_seq):
        pl.semaphore_signal(barrier, inc=1, device_id={"seq": lax.rem(me + d, n_seq)},
                            device_id_type=MESH)
    for d in range(1, n_tp):
        pl.semaphore_signal(barrier, inc=1, device_id={"tp": lax.rem(tp + d, n_tp)},
                            device_id_type=MESH)
    own_q = pltpu.make_async_copy(q, block(me), lsem.at[0])
    own_q.start()
    own_kv = pltpu.make_async_copy(kv, kva.at[me], lsem.at[1])
    own_kv.start()
    m_st[0] = jnp.full(m_st.shape[1:], NEGATIVE, jnp.float32)
    l_st[0] = jnp.zeros(l_st.shape[1:], jnp.float32)
    acc_st[0] = jnp.zeros(acc_st.shape[1:], jnp.float32)
    for r in range(n_req):
        last[r] = 0
    pl.semaphore_wait(barrier, n_seq + n_tp - 2)

    sent = []

    def send(*args):
        c = remote(*args)
        c.start()
        sent.append(c)

    for d in range(n_req - 1, 0, -1):
        send(q, block(me), qsem.at[d - 1], qrsem.at[me], {"seq": across(d)})
    for d in range(1, group):
        send(q, block(me), qsem.at[n_req - 2 + d], qrsem.at[me], {"seq": other(d)})
    def q_arrived(b):
        remote(q, block(b), qsem.at[0], qrsem.at[b], {"seq": other(1)}).wait_recv()

    def kv_arrived(b):
        remote(kv, kva.at[b], cssem.at[0], crsem.at[b], {"seq": other(1)}).wait_recv()

    for s in range(n_slots):
        pltpu.make_async_copy(pool.at[0, s], kbuf.at[s], ksem.at[s]).start()
        pltpu.make_async_copy(pool.at[1, s], vbuf.at[s], vsem.at[s]).start()
    loads = []
    for t in range(n_tp):
        c = pltpu.make_async_copy(weight.at[:, pl.ds(t * out_w, out_w)], wbuf.at[t], wsem.at[t])
        c.start()
        loads.append(c)
    zeros[...] = jnp.zeros(zeros.shape, zeros.dtype)
    writes = []
    for r in range(n_req):
        for c in range(2):
            writes.append(pltpu.make_async_copy(
                zeros, acc_kv.at[c, r, pl.ds(n_draft, zeros.shape[0])], zsem.at[r, c]))
            writes[-1].start()
    shape = table.shape
    number = (lax.broadcasted_iota(jnp.int32, shape, 0) * n_pages
              + lax.broadcasted_iota(jnp.int32, shape, 1) + 1)
    for s in range(n_slots):
        code[s] = jnp.sum(jnp.where(table[...] == me * n_slots + s, number, 0))

    for e in range(1, n_req):
        b = across(e)
        q_arrived(b)
        for d in range(1, group):
            send(block(b), block(b), fsem.at[(e - 1) * (group - 1) + d - 1], qrsem.at[b],
                 {"seq": other(d)})
    for d in range(1, group):
        send(kv, kva.at[me], cssem.at[n_req - 2 + d], crsem.at[me], {"seq": other(d)})
    for d in range(n_req - 1, 0, -1):
        send(kv, kva.at[me], cssem.at[d - 1], crsem.at[me], {"seq": across(d)})
    for d in range(1, group):
        q_arrived(other(d))
        for e in range(1, n_req):
            q_arrived(lax.rem(grp + e, n_req) * group + lax.rem(inner + d, group))
    own_q.wait()

    def forward(e, d, start):
        b = across(e)
        c = remote(kva.at[b], kva.at[b], cfsem.at[(e - 1) * (group - 1) + d - 1], crsem.at[b],
                   {"seq": other(d)})
        if start:
            c.start()
        else:
            c.wait_send()

    def step(s, carry):
        pltpu.make_async_copy(pool.at[0, s], kbuf.at[s], ksem.at[s]).wait()
        pltpu.make_async_copy(pool.at[1, s], vbuf.at[s], vsem.at[s]).wait()
        number = code[s]
        place = jnp.maximum(number - 1, 0)
        r = jnp.minimum(lax.div(place, n_pages), n_req - 1)
        left = jnp.where(number > 0, cache_len[r] - (place - r * n_pages) * page_len, 0)
        prev = last[r]
        scores = []
        for h in range(heads):
            cols = slice(h * HD, (h + 1) * HD)
            scores.append(lax.dot_general(
                qa[r, :, cols], kbuf[s, :, cols], NT, preferred_element_type=jnp.float32))
        live = lax.broadcasted_iota(jnp.int32, scores[0].shape, 1) < left
        probs = []
        scales = []
        for h in range(heads):
            x = jnp.where(live, scores[h] * scale, NEGATIVE)
            old = m_st[prev, h]
            new = jnp.maximum(old, jnp.max(x, axis=1, keepdims=True))
            p = jnp.exp(x - new)
            a = jnp.exp(old - new)
            m_st[s + 1, h] = new
            l_st[s + 1, h] = a * l_st[prev, h] + jnp.sum(p, axis=1, keepdims=True)
            probs.append(p.astype(jnp.bfloat16))
            scales.append(a)
        for h in range(heads):
            cols = slice(h * HD, (h + 1) * HD)
            o = jnp.dot(probs[h], vbuf[s, :, cols], preferred_element_type=jnp.float32)
            acc_st[s + 1, :, cols] = scales[h] * acc_st[prev, :, cols] + o
        for i in range(n_req):
            last[i] = jnp.where((left > 0) & (r == i), s + 1, last[i])
        return carry

    lax.fori_loop(0, n_slots, step, 0)

    lane = lax.broadcasted_iota(jnp.int32, (n_draft, HD), 1)
    for r in range(n_req):
        at = last[r]
        acc = acc_st[at].astype(jnp.bfloat16)
        info = jnp.zeros((n_draft, HD), jnp.float32)
        for h in range(heads):
            info = jnp.where(lane == h, m_st[at, h], info)
            info = jnp.where(lane == HD // 2 + h, l_st[at, h], info)
        for g in range(group):
            part[r * group + g] = acc[g * rows:(g + 1) * rows]
            stat[r * group + g] = info[g * rows:(g + 1) * rows]
    own_part = pltpu.make_async_copy(part.at[me], got.at[me], lsem.at[2])
    own_stat = pltpu.make_async_copy(stat.at[me], gstat.at[me], lsem.at[3])
    own_part.start()
    own_stat.start()
    for d in range(1, n_seq):
        peer = lax.rem(me + d, n_seq)
        send(stat.at[peer], gstat.at[me], tsem.at[d - 1], trsem.at[me], {"seq": peer})
        send(part.at[peer], got.at[me], asem.at[d - 1], arsem.at[me], {"seq": peer})

    for e in range(1, n_req):
        kv_arrived(across(e))
        for d in range(1, group):
            forward(e, d, True)

    own_kv.wait()
    for d in range(1, group):
        kv_arrived(other(d))
    allowed = mask[me] == 1
    mine = qa[grp, pl.ds(pl.multiple_of(inner * rows, rows), rows), :]
    tree_m = []
    tree_l = []
    for h in range(heads):
        cols = slice(h * HD, (h + 1) * HD)
        keys = jnp.concatenate([kva[grp * group + g, 0, :, cols] for g in range(group)], axis=0)
        values = jnp.concatenate([kva[grp * group + g, 1, :, cols] for g in range(group)], axis=0)
        x = lax.dot_general(mine[:, cols], keys, NT, preferred_element_type=jnp.float32) * scale
        x = jnp.where(allowed, x, NEGATIVE)
        top = jnp.max(x, axis=1, keepdims=True)
        p = jnp.where(allowed, jnp.exp(x - top), 0.0)
        tree_m.append(top)
        tree_l.append(jnp.sum(p, axis=1, keepdims=True))
        tree[:, cols] = jnp.dot(p.astype(jnp.bfloat16), values, preferred_element_type=jnp.float32)

    own_part.wait()
    own_stat.wait()
    for d in range(1, n_seq):
        i = lax.rem(me + n_seq - d, n_seq)
        remote(stat.at[i], gstat.at[i], tsem.at[d - 1], trsem.at[i], {"seq": i}).wait_recv()
        remote(part.at[i], got.at[i], asem.at[d - 1], arsem.at[i], {"seq": i}).wait_recv()
    for h in range(heads):
        cols = slice(h * HD, (h + 1) * HD)
        top = tree_m[h]
        for i in range(n_seq):
            top = jnp.maximum(top, gstat[i, :, h:h + 1])
        f = jnp.exp(tree_m[h] - top)
        den = f * tree_l[h]
        num = f * tree[:, cols]
        for i in range(n_seq):
            f = jnp.exp(gstat[i, :, h:h + 1] - top)
            den = den + f * gstat[i, :, HD // 2 + h:HD // 2 + h + 1]
            num = num + f * got[i, :, cols].astype(jnp.float32)
        att[:, cols] = (num / den).astype(jnp.bfloat16)
    for c in loads:
        c.wait()
    for d in range(1, n_tp):
        peer = lax.rem(tp + d, n_tp)
        pbuf[d - 1] = jnp.dot(att[...], wbuf[peer],
                              preferred_element_type=jnp.float32).astype(jnp.bfloat16)
        c = pltpu.make_async_remote_copy(
            src_ref=pbuf.at[d - 1], dst_ref=prbuf.at[d - 1], send_sem=psem.at[d - 1],
            recv_sem=prsem.at[d - 1], device_id={"tp": peer}, device_id_type=MESH)
        c.start()
        sent.append(c)
    total = jnp.dot(att[...], wbuf[tp], preferred_element_type=jnp.float32)
    for d in range(1, group):
        for e in range(1, n_req):
            kv_arrived(lax.rem(grp + e, n_req) * group + lax.rem(inner + d, group))
    for r in range(n_req):
        pick = (lax.broadcasted_iota(jnp.int32, (n_draft, n_draft), 0)
                == accepted[r:r + 1, :]).astype(jnp.bfloat16)
        for c in range(2):
            blocks = jnp.concatenate([kva[r * group + g, c] for g in range(group)], axis=0)
            picked[r, c] = lax.dot_general(
                pick, blocks, (((0,), (0,)), ((), ())),
                preferred_element_type=jnp.float32).astype(jnp.bfloat16)
            writes.append(pltpu.make_async_copy(
                picked.at[r, c], acc_kv.at[c, r, pl.ds(0, n_draft)], osem.at[r, c]))
            writes[-1].start()
    for d in range(1, n_tp):
        pltpu.make_async_remote_copy(
            src_ref=pbuf.at[d - 1], dst_ref=prbuf.at[d - 1], send_sem=psem.at[d - 1],
            recv_sem=prsem.at[d - 1], device_id={"tp": lax.rem(tp + d, n_tp)},
            device_id_type=MESH).wait_recv()
        total = total + prbuf[d - 1].astype(jnp.float32)
    out[...] = total.astype(out.dtype)
    for e in range(1, n_req):
        for d in range(1, group):
            forward(e, d, False)
    for c in writes:
        c.wait()
    for c in sent:
        c.wait_send()


def copy_kernel(accepted, layer, out, layer_out, held, held_layer, isem, osem):
    halves, n_req = accepted.shape[:2]
    parts = [(layer, held_layer, layer_out)]
    for c in range(halves):
        for r in range(n_req):
            parts.append((accepted.at[c, r], held.at[c, r], out.at[c, r]))
    loads = [pltpu.make_async_copy(a, b, isem.at[i]) for i, (a, b, _) in enumerate(parts)]
    stores = [pltpu.make_async_copy(b, c, osem.at[i]) for i, (_, b, c) in enumerate(parts)]
    for c in loads:
        c.start()
    for load, store in zip(loads, stores):
        load.wait()
        store.start()
    for c in stores:
        c.wait()


def body(draft_q, draft_kv, kv_pool, page_table, cache_len, tree_mask, accepted_rows, out_weight):
    n_seq = lax.axis_size("seq")
    n_tp = lax.axis_size("tp")
    rows, width = draft_q.shape
    heads = width // HD
    n_req, n_pages = page_table.shape
    n_draft = tree_mask.shape[1]
    n_slots, page_len = kv_pool.shape[1:3]
    group = n_seq // n_req
    out_w = out_weight.shape[1] // n_tp
    bf16, f32 = jnp.bfloat16, jnp.float32
    dma = pltpu.SemaphoreType.DMA

    layer, accepted_block = pl.pallas_call(
        functools.partial(fused_kernel, n_req, n_pages, n_seq, n_tp, group),
        out_shape=(jax.ShapeDtypeStruct((rows, out_w), bf16),
                   jax.ShapeDtypeStruct((2, n_req, page_len, width), bf16)),
        in_specs=[VMEM, SMEM, VMEM, VMEM, ANY, ANY, ANY, ANY],
        out_specs=(VMEM, ANY),
        scratch_shapes=[pltpu.VMEM((n_seq, 2, rows, width), bf16),
                        pltpu.VMEM((n_req, 2, n_draft, width), bf16),
                        pltpu.VMEM((page_len - n_draft, width), bf16),
                        pltpu.VMEM((n_req, n_draft, width), bf16),
                        pltpu.VMEM((n_slots, page_len, width), bf16),
                        pltpu.VMEM((n_slots, page_len, width), bf16),
                        pltpu.VMEM((n_slots + 1, heads, n_draft, HD), f32),
                        pltpu.VMEM((n_slots + 1, heads, n_draft, HD), f32),
                        pltpu.VMEM((n_slots + 1, n_draft, width), f32),
                        pltpu.VMEM((n_seq, rows, width), bf16),
                        pltpu.VMEM((n_seq, rows, HD), f32),
                        pltpu.VMEM((n_seq, rows, width), bf16),
                        pltpu.VMEM((n_seq, rows, HD), f32),
                        pltpu.VMEM((n_tp, width, out_w), bf16),
                        pltpu.VMEM((rows, width), bf16),
                        pltpu.VMEM((rows, width), f32),
                        pltpu.VMEM((n_tp - 1, rows, out_w), bf16),
                        pltpu.VMEM((n_tp - 1, rows, out_w), bf16),
                        pltpu.SMEM((n_req,), jnp.int32), pltpu.SMEM((n_slots,), jnp.int32),
                        dma((n_req + group - 2,)), dma((n_seq,)),
                        dma(((n_req - 1) * (group - 1),)),
                        dma((n_req + group - 2,)), dma((n_seq,)),
                        dma(((n_req - 1) * (group - 1),)),
                        dma((4,)), dma((n_slots,)), dma((n_slots,)), dma((n_req, 2)), dma((n_req, 2)),
                        dma((n_seq - 1,)), dma((n_seq,)), dma((n_seq - 1,)), dma((n_seq,)),
                        dma((n_tp,)), dma((n_tp - 1,)), dma((n_tp - 1,))],
        compiler_params=pltpu.CompilerParams(collective_id=0, has_side_effects=True,
                                             vmem_limit_bytes=58 << 20),
        cost_estimate=pl.CostEstimate(flops=10 ** 10, bytes_accessed=3 * 10 ** 7,
                                      transcendentals=10 ** 6),
    )(page_table, cache_len, tree_mask.reshape(n_seq, rows, n_draft), accepted_rows, draft_q, draft_kv, kv_pool,
      out_weight)

    accepted_kv, layer_out = pl.pallas_call(
        copy_kernel,
        out_shape=(jax.ShapeDtypeStruct((2, n_req, page_len, width), bf16),
                   jax.ShapeDtypeStruct((rows, out_w), bf16)),
        in_specs=[ANY, ANY],
        out_specs=(ANY, ANY),
        scratch_shapes=[pltpu.VMEM((2, n_req, page_len, width), bf16),
                        pltpu.VMEM((rows, out_w), bf16),
                        dma((2 * n_req + 1,)), dma((2 * n_req + 1,))],
        compiler_params=pltpu.CompilerParams(vmem_limit_bytes=58 << 20),
    )(accepted_block, layer)
    return (layer_out, accepted_kv)


def solution(mesh):
    return jax.shard_map(
        body,
        mesh=mesh,
        in_specs=(P("seq", "tp"), P(None, "seq", "tp"), P(None, "seq", None, "tp"),
                  P(), P(), P(), P(), P("tp", None)),
        out_specs=(P("seq", "tp"), P(None, None, None, "tp")),
        check_vma=False,
    )
```
